32 devices in a mesh: chan: 4 (over y, core), tm: 8 (over z, x).
Axes of the slice: x: 2, y: 2, z: 4, core: 2. Of those that a mesh axis runs over, the one named last changes fastest.
Arguments:
- readings: float32 [8192, 8192], P('chan', 'tm'), may hold values from -8 to 8
- channel_start: float32 [8192, 64], P(('chan', 'tm')), may hold values from -6 to 6
- time_start: float32 [8192, 64], P(('tm', 'chan')), may hold values from -0.75 to 0.75
Outputs:
- outliers: float32 [8192, 8192], P('chan', 'tm')
- channel_factors: float32 [8192, 64], P(('chan', 'tm'))
- time_factors: float32 [8192, 64], P(('tm', 'chan'))
The draws below stay inside these ranges and needn't reach their ends.
All inputs are finite; a program needn't handle non-finite values.
Results may differ from the reference program's by a relative error of at most 0.00019.
Values sent between devices are 32-bit elements; how exact they have to be, the bound alone decides.
A program may use at most 128 MiB of HBM per device.

```python
import jax
import jax.numpy as jnp
from jax import lax

RANK = 64
ITERS = 2
CHANNELS = 8192
TIMES = 8192


def levels(own_key, shape, pieces, low, top_value):
    factor_of, own = 1.0, jax.random.fold_in(own_key, 6)
    for axis_at, shards_of in pieces:
        heights = jnp.exp(jax.random.uniform(jax.random.fold_in(own, axis_at), (shards_of,), jnp.float32, low / len(pieces), top_value / len(pieces)))
        factor_of = factor_of * jnp.repeat(heights, shape[axis_at] // shards_of).reshape([-1 if axis == axis_at else 1 for axis in range(len(shape))])
    return factor_of


def centred(stream_key, dims, scale, bound, cuts=(), held_as=jnp.bfloat16):
    values = jax.random.normal(stream_key, dims, jnp.float32) * scale
    if len(cuts) > 0:
        values = levels(stream_key, dims, cuts, -0.22, 0.18) * values
    return jnp.clip(values, min=-bound, max=bound).astype(held_as)


def setup_inputs(seed: int = 0) -> dict:
    key_list = jax.random.split(jax.random.key(seed), 4)
    readings = centred(key_list[0], (CHANNELS, TIMES), 1.0, 8.0, ((0, 4), (1, 8)), jnp.float32)
    channel_start = centred(key_list[1], (CHANNELS, RANK), 1.0, 6.0, ((0, 32),), jnp.float32)
    time_start = centred(key_list[2], (TIMES, RANK), RANK ** -0.5, 0.75, ((0, 32),), jnp.float32)
    return dict(readings=readings, channel_start=channel_start, time_start=time_start)


threshold_level = 1.5
ridge_weight = 8.0

def product(first, second):
    return jnp.dot(first.astype(jnp.float32), second.astype(jnp.float32), precision=lax.Precision.HIGHEST, preferred_element_type=jnp.float32)

def solve_ridge(partial_value, gram):
    factor_chol = jnp.linalg.cholesky(gram)
    middle = lax.linalg.triangular_solve(factor_chol, partial_value, left_side=False, lower=True, transpose_a=True)
    return lax.linalg.triangular_solve(factor_chol, middle, left_side=False, lower=True, transpose_a=False)

def reference(readings, channel_start, time_start):
    identity = jnp.eye(RANK, dtype=jnp.float32)
    left_factor = channel_start
    right_factor = time_start
    outliers = readings
    for sweep in range(ITERS):
        residue = readings - product(left_factor, right_factor.T)
        outliers = residue - jnp.clip(residue, -threshold_level, threshold_level)
        cleaned = readings - outliers
        gram_right = product(right_factor.T, right_factor) + ridge_weight * identity
        left_factor = solve_ridge(product(cleaned, right_factor), gram_right)
        gram_left = product(left_factor.T, left_factor) + ridge_weight * identity
        right_factor = solve_ridge(product(cleaned.T, left_factor), gram_left)
    return (outliers, left_factor, right_factor)
```

```python
import functools

import jax
import jax.numpy as jnp
from jax import lax
from jax.experimental import pallas as pl
from jax.experimental.pallas import tpu as pltpu
from jax.sharding import PartitionSpec as P

ITERS = 2
LEVEL = 1.5
RIDGE = 8.0
LANES = 128
MESH = pl.DeviceIdType.MESH
HIGHEST = lax.Precision.HIGHEST


def split(value):
    high = value.astype(jnp.bfloat16)
    low = (value - high.astype(jnp.float32)).astype(jnp.bfloat16)
    return high, low


def stacked(value):
    high = value.astype(jnp.bfloat16).astype(jnp.float32)
    return jnp.concatenate([high, value - high], axis=0)


def dot(first, second):
    return jnp.dot(first, second, preferred_element_type=jnp.float32)


def solved(inv, value):
    return jnp.dot(inv, value, precision=HIGHEST, preferred_element_type=jnp.float32)


def outer_gram(value):
    return lax.dot_general(value, value, (((1,), (1,)), ((), ())), precision=HIGHEST,
                           preferred_element_type=jnp.float32)


def packed(gram):
    half = gram.shape[0] // 2
    return jnp.concatenate([gram[:half], gram[half:]], axis=1)


def unpacked(value):
    rank = value.shape[0] * 2
    return jnp.concatenate([value[:, :rank], value[:, rank:]], axis=0)


def pivots(gram, first_k, last_k):
    rank = gram.shape[0]
    rows = lax.broadcasted_iota(jnp.int32, (rank, rank), 0)
    cols = lax.broadcasted_iota(jnp.int32, (rank, rank), 1)
    lane = cols[:1]
    for k in range(first_k, last_k, 2):
        up, down = gram[k:k + 1, :], gram[k + 1:k + 2, :]
        first, second = gram[:, k:k + 1], gram[:, k + 1:k + 2]
        wide = lambda value: jnp.broadcast_to(value, (1, rank))
        p, q = wide(up[:, k:k + 1]), wide(up[:, k + 1:k + 2])
        r, d = wide(down[:, k:k + 1]), wide(down[:, k + 1:k + 2])
        inv = 1.0 / (p * d - q * r)
        up = jnp.where(lane == k, 1.0, jnp.where(lane == k + 1, 0.0, up))
        down = jnp.where(lane == k, 0.0, jnp.where(lane == k + 1, 1.0, down))
        new_up = (d * up - q * down) * inv
        new_down = (p * down - r * up) * inv
        rest = jnp.where((cols == k) | (cols == k + 1), 0.0, gram) - first * new_up - second * new_down
        gram = jnp.where(rows == k, new_up, jnp.where(rows == k + 1, new_down, rest))
    return gram


def kernel(n, m, cut, x_hbm, l_hbm, r_hbm, x, lout, rout,
           clean, lg, sbuf, precv, srecv, rg, tsend, tcore, tsum, grq, grsum, gl, glrecv,
           rcat, rwide, acc, inv_r, gacc,
           lz_s, lx_s, l_r, p_s, p_r, s_s, s_r, gq_s, gq_r, ga_s, ga_r, gl_s, gl_r,
           r_s, r_r, tc_s, tc_r, ty_s, ty_r, rc_s, rc_r, x_sem, in_sem):
    c = lax.axis_index("chan")
    t = lax.axis_index("tm")
    rank, lc = l_hbm.shape
    rc = r_hbm.shape[1]
    lk = lc // cut
    times = x.shape[1]
    width = times // 2
    half = n // 2
    z, pair = t // 2, t % 2
    other = z * 2 + 1 - pair
    ys = m // 2
    y, core = c // 2, c % 2
    twin = y * 2 + 1 - core

    def flip(s):
        value, bit = 0, 1
        while bit < half:
            value = value + bit * ((z // bit + s // bit) % 2)
            bit *= 2
        return value

    def side(own):
        return pair * own + (1 - pair) * (1 - own)

    def mine(q):
        return q * 2 + pair

    def theirs(q):
        return q * 2 + 1 - pair

    def peer_t(s):
        return lax.rem(t + s, n)

    def peer_c(s):
        return lax.rem(c + s, m)

    def peer_y(s):
        return lax.rem(y + s, ys)

    def copy_t(src, dst, ssem, rsem, j):
        return pltpu.make_async_remote_copy(src_ref=src, dst_ref=dst, send_sem=ssem, recv_sem=rsem,
                                            device_id=(c, j), device_id_type=MESH)

    def copy_c(src, dst, ssem, rsem, j):
        return pltpu.make_async_remote_copy(src_ref=src, dst_ref=dst, send_sem=ssem, recv_sem=rsem,
                                            device_id=(j, t), device_id_type=MESH)

    def loop(first, last, body):
        def step(s, carry):
            body(s)
            return carry
        lax.fori_loop(first, last, step, 0)

    def left_z(g, k, q, slot):
        return copy_t(lg.at[g, k, t], lg.at[g, k, slot], lz_s.at[g, k, q], l_r.at[g, k, slot], mine(q))

    def left_x(g, k, q, slot):
        return copy_t(lg.at[g, k, mine(q)], lg.at[g, k, slot], lx_s.at[g, k, q], l_r.at[g, k, slot], other)

    def left_send(g, k):
        loop(1, half, lambda s: left_z(g, k, flip(s), t).start())
        left_x(g, k, z, t).start()

    def left_own(g, k):
        def body(s):
            q = flip(s)
            left_z(g, k, q, mine(q)).wait_recv()
            left_x(g, k, q, mine(q)).start()
        loop(1, half, body)

    def left_other(g, k):
        loop(0, half, lambda s: left_x(g, k, s, theirs(s)).wait_recv())

    def pair_copy(i, k, q):
        return copy_t(sbuf.at[i, k, 0, q], precv.at[i, k, q], p_s.at[i, k, q], p_r.at[i, k, q], other)

    def pair_send(i, k):
        loop(0, half, lambda s: pair_copy(i, k, flip(half - 1 - s)).start())

    def s_copy(i, k, q, slot):
        return copy_t(sbuf.at[i, k, 1, q], srecv.at[i, k, slot], s_s.at[i, k, q], s_r.at[i, k, slot], mine(q))

    def join(i, k, s):
        q = flip(half - 1 - s)
        pair_copy(i, k, q).wait_recv()
        sbuf[i, k, 1, q] += precv[i, k, q]
        if s < half - 1:
            s_copy(i, k, q, z).start()

    def gq_copy(i, j, slot):
        return copy_t(grq.at[i, t, c], grq.at[i, slot, c], gq_s.at[i, j], gq_r.at[i, slot], j)

    def ga_copy(i, j, slot):
        return copy_c(grsum.at[i, c], grsum.at[i, slot], ga_s.at[i, j], ga_r.at[i, slot], j)

    def gl_copy(i, j, slot):
        return copy_c(gl.at[i], glrecv.at[i, slot], gl_s.at[i, j], gl_r.at[i, slot], j)

    def right_copy(j, slot):
        return copy_c(rg.at[0, c], rg.at[0, slot], r_s.at[j], r_r.at[slot], j)

    def tc_copy(i, q):
        return copy_c(tsend.at[i, q], tcore.at[i, q], tc_s.at[i, q], tc_r.at[i, q], twin)

    def ty_copy(i, q, to, slot):
        return copy_c(tsum.at[i, y, q], tsum.at[i, slot, q], ty_s.at[i, q, to], ty_r.at[i, q, slot],
                      to * 2 + core)

    def rc_copy(i, q, who):
        at = q * 2 + who
        return copy_c(rg.at[i, q * 2 + core], rg.at[i, at], rc_s.at[i, q], rc_r.at[i, q], twin)

    def x_copy(j):
        at = pl.ds(pl.multiple_of(j * lc, lc), lc)
        return pltpu.make_async_copy(x_hbm.at[at], x.at[at], x_sem.at[j])

    def l_in(k):
        return pltpu.make_async_copy(l_hbm.at[:, pl.ds(k * lk, lk)], lg.at[0, k, t], in_sem.at[k])

    def r_in():
        return pltpu.make_async_copy(r_hbm, rg.at[0, c], in_sem.at[cut])

    for k in range(cut):
        l_in(k).start()
    r_in().start()

    barrier = pltpu.get_barrier_semaphore()
    loop(1, n, lambda s: pl.semaphore_signal(barrier, inc=1, device_id=(c, peer_t(s)), device_id_type=MESH))
    loop(1, m, lambda s: pl.semaphore_signal(barrier, inc=1, device_id=(peer_c(s), t), device_id_type=MESH))

    loop(0, half, lambda s: x_copy(mine(s)).start())
    loop(0, half, lambda s: x_copy(theirs(s)).start())

    for k in range(cut):
        l_in(k).wait()
    r_in().wait()
    pl.semaphore_wait(barrier, n + m - 2)

    left_send(0, 0)
    loop(1, m, lambda s: right_copy(peer_c(s), c).start())
    for k in range(1, cut):
        left_send(0, k)

    rows = lax.broadcasted_iota(jnp.int32, (rank, rank), 0)
    cols = lax.broadcasted_iota(jnp.int32, (rank, rank), 1)
    ridge = jnp.where(rows == cols, RIDGE, 0.0).astype(jnp.float32)

    def when(cond, body):
        pl.when(cond)(body)

    for i in range(ITERS):
        last = i == ITERS - 1

        def prepare(q, total):
            part = rg[i, q]
            both = stacked(part)
            high = both[:rank]
            low = both[rank:]
            at = pl.ds(pl.multiple_of(q * rc, rc), rc)
            rcat[:, at] = jnp.concatenate([high, high, low, low], axis=0).astype(jnp.bfloat16)
            rwide[at, :] = both.T.astype(jnp.bfloat16)
            term = outer_gram(part)
            return term if total is None else total + term

        total = None
        if i == 0:
            left_own(0, 0)
            loop(1, m, lambda s: right_copy(c, peer_c(s)).wait_recv())
            for q in range(m):
                total = prepare(q, total)
        else:
            for q in range(ys):
                total = prepare(q * 2 + core, total)
            for q in range(ys):
                rc_copy(i, q, 1 - core).wait_recv()
                total = prepare(q * 2 + 1 - core, total)
        grq[i, t] = packed(total).reshape(m, rank // 2 // m, 2 * rank)
        loop(1, n, lambda s: gq_copy(i, peer_t(s), t).start())

        def share():
            loop(1, n, lambda s: gq_copy(i, t, peer_t(s)).wait_recv())
            value = grq[i, 0, c]
            for q in range(1, n):
                value = value + grq[i, q, c]
            grsum[i, c] = value
            loop(1, m, lambda s: ga_copy(i, peer_c(s), c).start())

        def block_a(k, own):
            js = [q * 2 + side(own) for q in range(half)]
            ats = [pl.ds(pl.multiple_of(j * lc + k * lk, lk), lk) for j in js]
            twos = [stacked(lg[i, k, j]).T.astype(jnp.bfloat16) for j in js]
            lcat = jnp.concatenate(twos, axis=0)
            lcat = jnp.concatenate([lcat, lcat], axis=1)
            deep = half * lk
            sums = None
            for b in range(times // width):
                part = pl.ds(b * width, width)
                values = jnp.concatenate([x[at, part] for at in ats], axis=0)
                low_rank = dot(lcat, rcat[:, part])
                residue = values - low_rank
                kept = jnp.clip(residue, -LEVEL, LEVEL)
                if last:
                    outlier = residue - kept
                    for q, at in enumerate(ats):
                        x[at, part] = outlier[q * lk:(q + 1) * lk]
                high, low = split(low_rank + kept)
                clean[0, k, own, :, part] = high
                clean[1, k, own, :, part] = low
                term = dot(jnp.concatenate([high, low], axis=0), rwide[part, :])
                sums = term if sums is None else sums + term
            flat = (sums[:deep] + sums[deep:]).T
            flat = flat[:rank] + flat[rank:]
            for q in range(half):
                sbuf[i, k, own, q] = flat[:, q * lk:(q + 1) * lk]

        if i == 0:
            def step_a(s, carry):
                k, own = s % cut, 1 - s // cut
                when((own == 1) & (k > 0), lambda: left_own(0, k))
                when(own == 0, lambda: left_other(0, k))
                when(k == 0, lambda: loop(0, half, lambda q: x_copy(q * 2 + side(own)).wait()))
                block_a(k, own)
                when(own == 0, lambda: pair_send(0, k))
                when((own == 1) & (k == cut - 1), share)
                return carry
            lax.fori_loop(0, 2 * cut, step_a, 0)
            joins = [(k, s) for k in range(cut) for s in range(half)]
        else:
            early = half // 2

            def step_a(s, carry):
                k, own = s // 2, s % 2
                block_a(k, own)
                when(own == 0, lambda: pair_send(i, k))

                @pl.when((own == 0) & (k == cut - 1))
                def _():
                    share()
                    for j in range(early):
                        join(i, 0, j)
                return carry
            lax.fori_loop(0, 2 * cut, step_a, 0)
            joins = [(k, s) for k in range(cut) for s in range(half) if (k, s) >= (0, early)]

        free = 0
        while free < len(joins) and joins[free][0] == 0 and i > 0:
            join(i, *joins[free])
            free += 1
        joins = joins[free:]
        loop(1, m, lambda s: ga_copy(i, c, peer_c(s)).wait_recv())
        gram = unpacked(grsum[i].reshape(rank // 2, 2 * rank)) + ridge
        per = max(2, rank // (len(joins) + 1) // 2 * 2)
        done = 0
        for k, s in joins:
            gram = pivots(gram, done, min(done + per, rank))
            done = min(done + per, rank)
            join(i, k, s)
        inv_r[...] = pivots(gram, done, rank)

        for k in range(cut):
            def add_s(s, value):
                q = flip(s)
                s_copy(i, k, z, q).wait_recv()
                return value + srecv[i, k, q]

            total = lax.fori_loop(1, half, add_s, sbuf[i, k, 1, z])
            piece = solved(inv_r[...], total)
            lg[i + 1, k, t] = piece
            left_send(i + 1, k)
            if last:
                lout[:, k * lk:(k + 1) * lk] = piece

        acc[...] = jnp.zeros_like(acc)
        gacc[...] = jnp.zeros_like(gacc)

        def send_gl():
            gram = packed(gacc[...])
            gl[i] = gram
            glrecv[i, c] = gram
            loop(1, m, lambda s: gl_copy(i, peer_c(s), c).start())

        def step_b(s, carry):
            k, own = s % cut, 1 - s // cut
            when(own == 1, lambda: left_own(i + 1, k))
            when(own == 0, lambda: left_other(i + 1, k))
            value = jnp.concatenate([lg[i + 1, k, q * 2 + side(own)] for q in range(half)], axis=1)
            gacc[...] += outer_gram(value)
            when(s == 2 * cut - 1, send_gl)
            both = stacked(value).astype(jnp.bfloat16)
            for b in range(times // width):
                part = pl.ds(b * width, width)
                acc[:, part] += dot(both, clean[0, k, own, :, part]) + dot(both, clean[1, k, own, :, part])
            return carry
        lax.fori_loop(0, 2 * cut, step_b, 0)

        def t_part(q, who):
            at = pl.ds(pl.multiple_of((q * 2 + who) * rc, rc), rc)
            return acc[:rank, at] + acc[rank:, at]

        def t_send(q):
            tsend[i, q] = t_part(q, 1 - core)
            tc_copy(i, q).start()

        def t_join(q):
            tsum[i, y, q] = t_part(q, core)
            tc_copy(i, q).wait_recv()
            tsum[i, y, q] += tcore[i, q]

        def over_y(s):
            q = peer_y(s)
            t_join(q)
            if last:
                when(s < ys, lambda: ty_copy(i, q, q, y).start())
            else:
                loop(1, ys, lambda v: ty_copy(i, q, peer_y(v), y).start())

        loop(1, ys + 1, lambda s: t_send(peer_y(s)))
        loop(1, ys + 1, over_y)

        loop(1, m, lambda s: gl_copy(i, c, peer_c(s)).wait_recv())
        total = glrecv[i, 0]
        for q in range(1, m):
            total = total + glrecv[i, q]
        inv_l = pivots(unpacked(total) + ridge, 0, rank)

        def total_of(q):
            value = tsum[i, 0, q]
            for v in range(1, ys):
                value = value + tsum[i, v, q]
            return value

        if last:
            loop(1, ys, lambda s: ty_copy(i, y, y, peer_y(s)).wait_recv())
            rout[...] = solved(inv_l, total_of(y))
        else:
            for q in range(ys):
                loop(1, ys, lambda s: ty_copy(i, q, y, peer_y(s)).wait_recv())
                rg[i + 1, q * 2 + core] = solved(inv_l, total_of(q))
                rc_copy(i + 1, q, core).start()

    loop(1, m, lambda s: right_copy(peer_c(s), c).wait_send())
    for i in range(ITERS):
        for k in range(cut):
            loop(0, half, lambda s: pair_copy(i, k, s).wait_send())
            loop(1, half, lambda s: s_copy(i, k, flip(s), z).wait_send())
        loop(1, n, lambda s: gq_copy(i, peer_t(s), t).wait_send())
        loop(1, m, lambda s: ga_copy(i, peer_c(s), c).wait_send())
        loop(1, m, lambda s: gl_copy(i, peer_c(s), c).wait_send())
        loop(0, ys, lambda q: tc_copy(i, q).wait_send())
        if i == ITERS - 1:
            loop(1, ys, lambda s: ty_copy(i, peer_y(s), peer_y(s), y).wait_send())
        else:
            for q in range(ys):
                loop(1, ys, lambda s: ty_copy(i, q, peer_y(s), y).wait_send())
            loop(0, ys, lambda q: rc_copy(i + 1, q, core).wait_send())
    for g in range(ITERS + 1):
        for k in range(cut):
            loop(1, half, lambda s: left_z(g, k, flip(s), t).wait_send())
            loop(0, half, lambda s: left_x(g, k, s, t).wait_send())


def shards(n, m, readings, channel_start, time_start):
    lc, rank = channel_start.shape
    rc = time_start.shape[0]
    rows, times = readings.shape
    cut = max(1, lc // LANES)
    lk, half, ys = lc // cut, n // 2, m // 2
    f32 = jnp.float32
    vmem = pl.BlockSpec(memory_space=pltpu.VMEM)
    hbm = pl.BlockSpec(memory_space=pltpu.HBM)
    dma = pltpu.SemaphoreType.DMA
    outliers, left, right = pl.pallas_call(
        functools.partial(kernel, n, m, cut),
        out_shape=(jax.ShapeDtypeStruct((rows, times), f32),
                   jax.ShapeDtypeStruct((rank, lc), f32),
                   jax.ShapeDtypeStruct((rank, rc), f32)),
        in_specs=[hbm, hbm, hbm],
        out_specs=(vmem, vmem, vmem),
        scratch_shapes=[
            pltpu.VMEM((2, cut, 2, half * lk, times), jnp.bfloat16),
            pltpu.VMEM((ITERS + 1, cut, n, rank, lk), f32),
            pltpu.VMEM((ITERS, cut, 2, half, rank, lk), f32),
            pltpu.VMEM((ITERS, cut, half, rank, lk), f32),
            pltpu.VMEM((ITERS, cut, half, rank, lk), f32),
            pltpu.VMEM((ITERS, m, rank, rc), f32),
            pltpu.VMEM((ITERS, ys, rank, rc), f32),
            pltpu.VMEM((ITERS, ys, rank, rc), f32),
            pltpu.VMEM((ITERS, ys, ys, rank, rc), f32),
            pltpu.VMEM((ITERS, n, m, rank // 2 // m, 2 * rank), f32),
            pltpu.VMEM((ITERS, m, rank // 2 // m, 2 * rank), f32),
            pltpu.VMEM((ITERS, rank // 2, 2 * rank), f32),
            pltpu.VMEM((ITERS, m, rank // 2, 2 * rank), f32),
            pltpu.VMEM((4 * rank, times), jnp.bfloat16),
            pltpu.VMEM((times, 2 * rank), jnp.bfloat16),
            pltpu.VMEM((2 * rank, times), f32),
            pltpu.VMEM((rank, rank), f32),
            pltpu.VMEM((rank, rank), f32),
            dma((ITERS + 1, cut, half)), dma((ITERS + 1, cut, half)), dma((ITERS + 1, cut, n)),
            dma((ITERS, cut, half)), dma((ITERS, cut, half)),
            dma((ITERS, cut, half)), dma((ITERS, cut, half)),
            dma((ITERS, n)), dma((ITERS, n)),
            dma((ITERS, m)), dma((ITERS, m)),
            dma((ITERS, m)), dma((ITERS, m)),
            dma((m,)), dma((m,)),
            dma((ITERS, ys)), dma((ITERS, ys)),
            dma((ITERS, ys, ys)), dma((ITERS, ys, ys)),
            dma((ITERS, ys)), dma((ITERS, ys)),
            dma((n,)), dma((cut + 1,)),
        ],
        compiler_params=pltpu.CompilerParams(collective_id=0, has_side_effects=True,
                                             vmem_limit_bytes=42 * 1024 * 1024),
    )(readings, channel_start.T, time_start.T)
    return outliers, left.T, right.T


def solution(mesh):
    n, m = mesh.shape["tm"], mesh.shape["chan"]
    specs = (P("chan", "tm"), P(("chan", "tm"), None), P(("tm", "chan"), None))
    return jax.shard_map(functools.partial(shards, n, m), mesh=mesh, in_specs=specs, out_specs=specs,
                         check_vma=False)
```

```python
import functools

import jax
import jax.numpy as jnp
from jax import lax
from jax.experimental import pallas as pl
from jax.experimental.pallas import tpu as pltpu
from jax.sharding import PartitionSpec as P

ITERS = 2
LEVEL = 1.5
RIDGE = 8.0
LANES = 128
MESH = pl.DeviceIdType.MESH
HIGHEST = lax.Precision.HIGHEST


def split(value):
    high = value.astype(jnp.bfloat16)
    low = (value - high.astype(jnp.float32)).astype(jnp.bfloat16)
    return high, low


def stacked(value):
    high = value.astype(jnp.bfloat16).astype(jnp.float32)
    return jnp.concatenate([high, value - high], axis=0)


def dot(first, second):
    return jnp.dot(first, second, preferred_element_type=jnp.float32)


def solved(inv, value):
    return jnp.dot(inv, value, precision=HIGHEST, preferred_element_type=jnp.float32)


def outer_gram(value):
    return lax.dot_general(value, value, (((1,), (1,)), ((), ())), precision=HIGHEST,
                           preferred_element_type=jnp.float32)


def packed(gram):
    half = gram.shape[0] // 2
    return jnp.concatenate([gram[:half], gram[half:]], axis=1)


def unpacked(value):
    rank = value.shape[0] * 2
    return jnp.concatenate([value[:, :rank], value[:, rank:]], axis=0)


def pivots(gram, first_k, last_k):
    rank = gram.shape[0]
    rows = lax.broadcasted_iota(jnp.int32, (rank, rank), 0)
    cols = lax.broadcasted_iota(jnp.int32, (rank, rank), 1)
    lane = cols[:1]
    for k in range(first_k, last_k, 2):
        up, down = gram[k:k + 1, :], gram[k + 1:k + 2, :]
        first, second = gram[:, k:k + 1], gram[:, k + 1:k + 2]
        wide = lambda value: jnp.broadcast_to(value, (1, rank))
        p, q = wide(up[:, k:k + 1]), wide(up[:, k + 1:k + 2])
        r, d = wide(down[:, k:k + 1]), wide(down[:, k + 1:k + 2])
        inv = 1.0 / (p * d - q * r)
        up = jnp.where(lane == k, 1.0, jnp.where(lane == k + 1, 0.0, up))
        down = jnp.where(lane == k, 0.0, jnp.where(lane == k + 1, 1.0, down))
        new_up = (d * up - q * down) * inv
        new_down = (p * down - r * up) * inv
        rest = jnp.where((cols == k) | (cols == k + 1), 0.0, gram) - first * new_up - second * new_down
        gram = jnp.where(rows == k, new_up, jnp.where(rows == k + 1, new_down, rest))
    return gram


def kernel(n, m, cut, rc, x_hbm, starts, x, lout, rout,
           clean, lg, sbuf, precv, srecv, rg, tsend, tcore, tsum, grq, grsum, glq, glsum, glall,
           rcat, rwide, acc, inv_r,
           lz_s, lx_s, l_r, p_s, p_r, s_s, s_r, gq_s, gq_r, ga_s, ga_r, hq_s, hq_r, ht_s, ht_r, ha_s, ha_r,
           r_s, r_r, tc_s, tc_r, ty_s, ty_r, rc_s, rc_r, x_sem):
    c = lax.axis_index("chan")
    t = lax.axis_index("tm")
    rank = starts.shape[0]
    lc = starts.shape[1] - rc
    lk = lc // cut
    times = x.shape[1]
    width = times // 2
    half = n // 2
    z, pair = t // 2, t % 2
    other = z * 2 + 1 - pair
    ys = m // 2
    y, core = c // 2, c % 2
    twin = y * 2 + 1 - core

    def flip(s):
        value, bit = 0, 1
        while bit < half:
            value = value + bit * ((z // bit + s // bit) % 2)
            bit *= 2
        return value

    def side(own):
        return pair * own + (1 - pair) * (1 - own)

    def mine(q):
        return q * 2 + pair

    def theirs(q):
        return q * 2 + 1 - pair

    def peer_t(s):
        return lax.rem(t + s, n)

    def peer_c(s):
        return lax.rem(c + s, m)

    def peer_y(s):
        return lax.rem(y + s, ys)

    def copy_t(src, dst, ssem, rsem, j):
        return pltpu.make_async_remote_copy(src_ref=src, dst_ref=dst, send_sem=ssem, recv_sem=rsem,
                                            device_id=(c, j), device_id_type=MESH)

    def copy_c(src, dst, ssem, rsem, j):
        return pltpu.make_async_remote_copy(src_ref=src, dst_ref=dst, send_sem=ssem, recv_sem=rsem,
                                            device_id=(j, t), device_id_type=MESH)

    def loop(first, last, body):
        def step(s, carry):
            body(s)
            return carry
        lax.fori_loop(first, last, step, 0)

    def left_mine(g, k):
        return starts.at[:, pl.ds(k * lk, lk)] if g == 0 else lg.at[g, k, t]

    def left_z(g, k, q, slot):
        return copy_t(left_mine(g, k), lg.at[g, k, slot], lz_s.at[g, k, q], l_r.at[g, k, slot], mine(q))

    def left_x(g, k, q, slot, own=False):
        return copy_t(left_mine(g, k) if own else lg.at[g, k, mine(q)], lg.at[g, k, slot], lx_s.at[g, k, q], l_r.at[g, k, slot], other)

    def left_send(g, k):
        loop(1, half, lambda s: left_z(g, k, flip(s), t).start())
        left_x(g, k, z, t, True).start()

    def left_own(g, k):
        def body(s):
            q = flip(s)
            left_z(g, k, q, mine(q)).wait_recv()
            left_x(g, k, q, mine(q)).start()
        loop(1, half, body)

    def left_other(g, k):
        loop(0, half, lambda s: left_x(g, k, s, theirs(s)).wait_recv())

    def pair_copy(i, k, q):
        return copy_t(sbuf.at[i, k, 0, q], precv.at[i, k, q], p_s.at[i, k, q], p_r.at[i, k, q], other)

    def pair_send(i, k):
        loop(0, half, lambda s: pair_copy(i, k, flip(half - 1 - s)).start())

    def s_copy(i, k, q, slot):
        return copy_t(sbuf.at[i, k, 1, q], srecv.at[i, k, slot], s_s.at[i, k, q], s_r.at[i, k, slot], mine(q))

    def join(i, k, s):
        q = flip(half - 1 - s)
        pair_copy(i, k, q).wait_recv()
        sbuf[i, k, 1, q] += precv[i, k, q]
        if s < half - 1:
            s_copy(i, k, q, z).start()

    def gq_copy(i, j, slot):
        return copy_t(grq.at[i, t, c], grq.at[i, slot, c], gq_s.at[i, j], gq_r.at[i, slot], j)

    def ga_copy(i, j, slot):
        return copy_c(grsum.at[i, c], grsum.at[i, slot], ga_s.at[i, j], ga_r.at[i, slot], j)

    def hq_copy(i, j, slot):
        return copy_c(glq.at[i, c, j], glq.at[i, slot, j], hq_s.at[i, j], hq_r.at[i, slot], j)

    def ht_copy(i, j, slot):
        return copy_t(glsum.at[i, t], glsum.at[i, slot], ht_s.at[i, j], ht_r.at[i, slot], j)

    def ha_copy(i, j, slot):
        return copy_c(glall.at[i, c], glall.at[i, slot], ha_s.at[i, j], ha_r.at[i, slot], j)

    def right_copy(j, slot):
        return copy_c(starts.at[:, pl.ds(lc, rc)], rg.at[0, slot], r_s.at[j], r_r.at[slot], j)

    def tc_copy(i, q):
        return copy_c(tsend.at[i, q], tcore.at[i, q], tc_s.at[i, q], tc_r.at[i, q], twin)

    def ty_copy(i, q, to, slot):
        return copy_c(tsum.at[i, y, q], tsum.at[i, slot, q], ty_s.at[i, q, to], ty_r.at[i, q, slot],
                      to * 2 + core)

    def rc_copy(i, q, who):
        at = q * 2 + who
        return copy_c(rg.at[i, q * 2 + core], rg.at[i, at], rc_s.at[i, q], rc_r.at[i, q], twin)

    def x_copy(j):
        at = pl.ds(pl.multiple_of(j * lc, lc), lc)
        return pltpu.make_async_copy(x_hbm.at[at], x.at[at], x_sem.at[j])

    barrier = pltpu.get_barrier_semaphore()
    loop(1, n, lambda s: pl.semaphore_signal(barrier, inc=1, device_id=(c, peer_t(s)), device_id_type=MESH))
    loop(1, m, lambda s: pl.semaphore_signal(barrier, inc=1, device_id=(peer_c(s), t), device_id_type=MESH))

    pl.semaphore_wait(barrier, n + m - 2)

    left_send(0, 0)
    loop(1, m, lambda s: right_copy(peer_c(s), c).start())
    for k in range(1, cut):
        left_send(0, k)
    loop(0, half, lambda s: x_copy(mine(s)).start())
    loop(0, half, lambda s: x_copy(theirs(s)).start())
    for k in range(cut):
        lg[0, k, t] = starts[:, k * lk:(k + 1) * lk]
    rg[0, c] = starts[:, lc:]

    rows = lax.broadcasted_iota(jnp.int32, (rank, rank), 0)
    cols = lax.broadcasted_iota(jnp.int32, (rank, rank), 1)
    ridge = jnp.where(rows == cols, RIDGE, 0.0).astype(jnp.float32)

    def when(cond, body):
        pl.when(cond)(body)

    for i in range(ITERS):
        last = i == ITERS - 1

        def prepare(q, total):
            part = rg[i, q]
            both = stacked(part)
            high = both[:rank]
            low = both[rank:]
            at = pl.ds(pl.multiple_of(q * rc, rc), rc)
            rcat[:, at] = jnp.concatenate([high, high, low, low], axis=0).astype(jnp.bfloat16)
            rwide[at, :] = both.T.astype(jnp.bfloat16)
            term = outer_gram(part)
            return term if total is None else total + term

        total = None
        if i == 0:
            left_own(0, 0)
            loop(1, m, lambda s: right_copy(c, peer_c(s)).wait_recv())
            for q in range(m):
                total = prepare(q, total)
        else:
            for q in range(ys):
                total = prepare(q * 2 + core, total)
            for q in range(ys):
                rc_copy(i, q, 1 - core).wait_recv()
                total = prepare(q * 2 + 1 - core, total)
        grq[i, t] = packed(total).reshape(m, rank // 2 // m, 2 * rank)
        loop(1, n, lambda s: gq_copy(i, peer_t(s), t).start())

        def share():
            loop(1, n, lambda s: gq_copy(i, t, peer_t(s)).wait_recv())
            value = grq[i, 0, c]
            for q in range(1, n):
                value = value + grq[i, q, c]
            grsum[i, c] = value
            loop(1, m, lambda s: ga_copy(i, peer_c(s), c).start())

        def block_a(k, own):
            js = [q * 2 + side(own) for q in range(half)]
            ats = [pl.ds(pl.multiple_of(j * lc + k * lk, lk), lk) for j in js]
            twos = [stacked(lg[i, k, j]).T.astype(jnp.bfloat16) for j in js]
            lcat = jnp.concatenate(twos, axis=0)
            lcat = jnp.concatenate([lcat, lcat], axis=1)
            deep = half * lk
            sums = None
            for b in range(times // width):
                part = pl.ds(b * width, width)
                values = jnp.concatenate([x[at, part] for at in ats], axis=0)
                low_rank = dot(lcat, rcat[:, part])
                residue = values - low_rank
                kept = jnp.clip(residue, -LEVEL, LEVEL)
                if last:
                    outlier = residue - kept
                    for q, at in enumerate(ats):
                        x[at, part] = outlier[q * lk:(q + 1) * lk]
                high, low = split(low_rank + kept)
                clean[0, k, own, :, part] = high
                clean[1, k, own, :, part] = low
                term = dot(jnp.concatenate([high, low], axis=0), rwide[part, :])
                sums = term if sums is None else sums + term
            flat = (sums[:deep] + sums[deep:]).T
            flat = flat[:rank] + flat[rank:]
            for q in range(half):
                sbuf[i, k, own, q] = flat[:, q * lk:(q + 1) * lk]

        if i == 0:
            def step_a(s, carry):
                k, own = s % cut, 1 - s // cut
                when((own == 1) & (k > 0), lambda: left_own(0, k))
                when(own == 0, lambda: left_other(0, k))
                when(k == 0, lambda: loop(0, half, lambda q: x_copy(q * 2 + side(own)).wait()))
                block_a(k, own)
                when(own == 0, lambda: pair_send(0, k))
                when((own == 1) & (k == cut - 1), share)
                return carry
            lax.fori_loop(0, 2 * cut, step_a, 0)
            joins = [(k, s) for k in range(cut) for s in range(half)]
        else:
            early = half // 2

            def step_a(s, carry):
                k, own = s // 2, s % 2
                block_a(k, own)
                when(own == 0, lambda: pair_send(i, k))

                @pl.when((own == 0) & (k == cut - 1))
                def _():
                    share()
                    for j in range(early):
                        join(i, 0, j)
                return carry
            lax.fori_loop(0, 2 * cut, step_a, 0)
            joins = [(k, s) for k in range(cut) for s in range(half) if (k, s) >= (0, early)]

        free = 0
        while free < len(joins) and joins[free][0] == 0 and i > 0:
            join(i, *joins[free])
            free += 1
        joins = joins[free:]
        loop(1, m, lambda s: ga_copy(i, c, peer_c(s)).wait_recv())
        gram = unpacked(grsum[i].reshape(rank // 2, 2 * rank)) + ridge
        per = max(2, rank // (len(joins) + 1) // 2 * 2)
        done = 0
        for k, s in joins:
            gram = pivots(gram, done, min(done + per, rank))
            done = min(done + per, rank)
            join(i, k, s)
        inv_r[...] = pivots(gram, done, rank)

        for k in range(cut):
            def add_s(s, value):
                q = flip(s)
                s_copy(i, k, z, q).wait_recv()
                return value + srecv[i, k, q]

            total = lax.fori_loop(1, half, add_s, sbuf[i, k, 1, z])
            piece = solved(inv_r[...], total)
            lg[i + 1, k, t] = piece
            left_send(i + 1, k)
            term = outer_gram(piece)
            gram = term if k == 0 else gram + term
            if last:
                lout[:, k * lk:(k + 1) * lk] = piece

        glq[i, c] = packed(gram).reshape(m, rank // 2 // m, 2 * rank)
        loop(1, m, lambda s: hq_copy(i, peer_c(s), c).start())
        acc[...] = jnp.zeros_like(acc)

        def share_chan():
            loop(1, m, lambda s: hq_copy(i, c, peer_c(s)).wait_recv())
            value = glq[i, 0, c]
            for q in range(1, m):
                value = value + glq[i, q, c]
            glsum[i, t] = value
            loop(1, n, lambda s: ht_copy(i, peer_t(s), t).start())

        def share_tm():
            loop(1, n, lambda s: ht_copy(i, t, peer_t(s)).wait_recv())
            value = glsum[i, 0]
            for q in range(1, n):
                value = value + glsum[i, q]
            glall[i, c] = value
            loop(1, m, lambda s: ha_copy(i, peer_c(s), c).start())

        def step_b(s, carry):
            k, own = s % cut, 1 - s // cut
            when(own == 1, lambda: left_own(i + 1, k))
            when(own == 0, lambda: left_other(i + 1, k))
            value = jnp.concatenate([lg[i + 1, k, q * 2 + side(own)] for q in range(half)], axis=1)
            both = stacked(value).astype(jnp.bfloat16)
            for b in range(times // width):
                part = pl.ds(b * width, width)
                acc[:, part] += dot(both, clean[0, k, own, :, part]) + dot(both, clean[1, k, own, :, part])
            when(s == 0, share_chan)
            when(s == cut, share_tm)
            return carry
        lax.fori_loop(0, 2 * cut, step_b, 0)

        def t_part(q, who):
            at = pl.ds(pl.multiple_of((q * 2 + who) * rc, rc), rc)
            return acc[:rank, at] + acc[rank:, at]

        def t_send(q):
            tsend[i, q] = t_part(q, 1 - core)
            tc_copy(i, q).start()

        def t_join(q):
            tsum[i, y, q] = t_part(q, core)
            tc_copy(i, q).wait_recv()
            tsum[i, y, q] += tcore[i, q]

        def over_y(s):
            q = peer_y(s)
            t_join(q)
            if last:
                when(s < ys, lambda: ty_copy(i, q, q, y).start())
            else:
                loop(1, ys, lambda v: ty_copy(i, q, peer_y(v), y).start())

        loop(1, ys + 1, lambda s: t_send(peer_y(s)))
        loop(1, ys + 1, over_y)

        loop(1, m, lambda s: ha_copy(i, c, peer_c(s)).wait_recv())
        inv_l = pivots(unpacked(glall[i].reshape(rank // 2, 2 * rank)) + ridge, 0, rank)

        def total_of(q):
            value = tsum[i, 0, q]
            for v in range(1, ys):
                value = value + tsum[i, v, q]
            return value

        if last:
            loop(1, ys, lambda s: ty_copy(i, y, y, peer_y(s)).wait_recv())
            rout[...] = solved(inv_l, total_of(y))
        else:
            for q in range(ys):
                loop(1, ys, lambda s: ty_copy(i, q, y, peer_y(s)).wait_recv())
                rg[i + 1, q * 2 + core] = solved(inv_l, total_of(q))
                rc_copy(i + 1, q, core).start()

    loop(1, m, lambda s: right_copy(peer_c(s), c).wait_send())
    for i in range(ITERS):
        for k in range(cut):
            loop(0, half, lambda s: pair_copy(i, k, s).wait_send())
            loop(1, half, lambda s: s_copy(i, k, flip(s), z).wait_send())
        loop(1, n, lambda s: gq_copy(i, peer_t(s), t).wait_send())
        loop(1, m, lambda s: ga_copy(i, peer_c(s), c).wait_send())
        loop(1, m, lambda s: hq_copy(i, peer_c(s), c).wait_send())
        loop(1, n, lambda s: ht_copy(i, peer_t(s), t).wait_send())
        loop(1, m, lambda s: ha_copy(i, peer_c(s), c).wait_send())
        loop(0, ys, lambda q: tc_copy(i, q).wait_send())
        if i == ITERS - 1:
            loop(1, ys, lambda s: ty_copy(i, peer_y(s), peer_y(s), y).wait_send())
        else:
            for q in range(ys):
                loop(1, ys, lambda s: ty_copy(i, q, peer_y(s), y).wait_send())
            loop(0, ys, lambda q: rc_copy(i + 1, q, core).wait_send())
    for g in range(ITERS + 1):
        for k in range(cut):
            loop(1, half, lambda s: left_z(g, k, flip(s), t).wait_send())
            loop(0, half, lambda s: left_x(g, k, s, t).wait_send())


def store(parts, x, left, right, x_out, left_out, right_out, sem):
    rows = x.shape[0] // parts
    copies = [pltpu.make_async_copy(left, left_out, sem.at[parts]),
              pltpu.make_async_copy(right, right_out, sem.at[parts + 1])]
    for q in range(parts):
        at = pl.ds(q * rows, rows)
        copies.append(pltpu.make_async_copy(x.at[at], x_out.at[at], sem.at[q]))
    for copy in copies:
        copy.start()
    for copy in copies:
        copy.wait()


def shards(n, m, readings, channel_start, time_start):
    lc, rank = channel_start.shape
    rc = time_start.shape[0]
    rows, times = readings.shape
    cut = max(1, lc // LANES)
    lk, half, ys = lc // cut, n // 2, m // 2
    f32 = jnp.float32
    vmem = pl.BlockSpec(memory_space=pltpu.VMEM)
    hbm = pl.BlockSpec(memory_space=pltpu.HBM)
    dma = pltpu.SemaphoreType.DMA
    outliers, left, right = pl.pallas_call(
        functools.partial(kernel, n, m, cut, rc),
        out_shape=(jax.ShapeDtypeStruct((rows, times), f32),
                   jax.ShapeDtypeStruct((rank, lc), f32),
                   jax.ShapeDtypeStruct((rank, rc), f32)),
        in_specs=[hbm, vmem],
        out_specs=(vmem, vmem, vmem),
        scratch_shapes=[
            pltpu.VMEM((2, cut, 2, half * lk, times), jnp.bfloat16),
            pltpu.VMEM((ITERS + 1, cut, n, rank, lk), f32),
            pltpu.VMEM((ITERS, cut, 2, half, rank, lk), f32),
            pltpu.VMEM((ITERS, cut, half, rank, lk), f32),
            pltpu.VMEM((ITERS, cut, half, rank, lk), f32),
            pltpu.VMEM((ITERS, m, rank, rc), f32),
            pltpu.VMEM((ITERS, ys, rank, rc), f32),
            pltpu.VMEM((ITERS, ys, rank, rc), f32),
            pltpu.VMEM((ITERS, ys, ys, rank, rc), f32),
            pltpu.VMEM((ITERS, n, m, rank // 2 // m, 2 * rank), f32),
            pltpu.VMEM((ITERS, m, rank // 2 // m, 2 * rank), f32),
            pltpu.VMEM((ITERS, m, m, rank // 2 // m, 2 * rank), f32),
            pltpu.VMEM((ITERS, n, rank // 2 // m, 2 * rank), f32),
            pltpu.VMEM((ITERS, m, rank // 2 // m, 2 * rank), f32),
            pltpu.VMEM((4 * rank, times), jnp.bfloat16),
            pltpu.VMEM((times, 2 * rank), jnp.bfloat16),
            pltpu.VMEM((2 * rank, times), f32),
            pltpu.VMEM((rank, rank), f32),
            dma((ITERS + 1, cut, half)), dma((ITERS + 1, cut, half)), dma((ITERS + 1, cut, n)),
            dma((ITERS, cut, half)), dma((ITERS, cut, half)),
            dma((ITERS, cut, half)), dma((ITERS, cut, half)),
            dma((ITERS, n)), dma((ITERS, n)),
            dma((ITERS, m)), dma((ITERS, m)),
            dma((ITERS, m)), dma((ITERS, m)),
            dma((ITERS, n)), dma((ITERS, n)),
            dma((ITERS, m)), dma((ITERS, m)),
            dma((m,)), dma((m,)),
            dma((ITERS, ys)), dma((ITERS, ys)),
            dma((ITERS, ys, ys)), dma((ITERS, ys, ys)),
            dma((ITERS, ys)), dma((ITERS, ys)),
            dma((n,)),
        ],
        compiler_params=pltpu.CompilerParams(collective_id=0, has_side_effects=True,
                                             vmem_limit_bytes=42 * 1024 * 1024),
    )(readings, jnp.concatenate([channel_start.T, time_start.T], axis=1))
    parts = 8
    outliers, left, right = pl.pallas_call(
        functools.partial(store, parts),
        out_shape=(jax.ShapeDtypeStruct((rows, times), f32),
                   jax.ShapeDtypeStruct((rank, lc), f32),
                   jax.ShapeDtypeStruct((rank, rc), f32)),
        in_specs=[pl.BlockSpec(memory_space=pl.ANY)] * 3,
        out_specs=(hbm, hbm, hbm),
        scratch_shapes=[dma((parts + 2,))],
        compiler_params=pltpu.CompilerParams(vmem_limit_bytes=4 * 1024 * 1024),
    )(outliers, left, right)
    return outliers, left.T, right.T


def solution(mesh):
    n, m = mesh.shape["tm"], mesh.shape["chan"]
    specs = (P("chan", "tm"), P(("chan", "tm"), None), P(("tm", "chan"), None))
    return jax.shard_map(functools.partial(shards, n, m), mesh=mesh, in_specs=specs, out_specs=specs,
                         check_vma=False)
```

```python
import functools

import jax
import jax.numpy as jnp
from jax import lax
from jax.experimental import pallas as pl
from jax.experimental.pallas import tpu as pltpu
from jax.sharding import PartitionSpec as P

ITERS = 2
LEVEL = 1.5
RIDGE = 8.0
LANES = 128
MESH = pl.DeviceIdType.MESH
HIGHEST = lax.Precision.HIGHEST


def split(value):
    high = value.astype(jnp.bfloat16)
    low = (value - high.astype(jnp.float32)).astype(jnp.bfloat16)
    return high, low


def stacked(value):
    high = value.astype(jnp.bfloat16).astype(jnp.float32)
    return jnp.concatenate([high, value - high], axis=0)


def dot(first, second):
    return jnp.dot(first, second, preferred_element_type=jnp.float32)


def solved(inv, value):
    return jnp.dot(inv, value, precision=HIGHEST, preferred_element_type=jnp.float32)


def outer_gram(value):
    return lax.dot_general(value, value, (((1,), (1,)), ((), ())), precision=HIGHEST,
                           preferred_element_type=jnp.float32)


def packed(gram):
    half = gram.shape[0] // 2
    return jnp.concatenate([gram[:half], gram[half:]], axis=1)


def unpacked(value):
    rank = value.shape[0] * 2
    return jnp.concatenate([value[:, :rank], value[:, rank:]], axis=0)


def pivots(gram, first_k, last_k):
    rank = gram.shape[0]
    rows = lax.broadcasted_iota(jnp.int32, (rank, rank), 0)
    cols = lax.broadcasted_iota(jnp.int32, (rank, rank), 1)
    lane = cols[:1]
    wide = lambda value: jnp.broadcast_to(value, (1, rank))
    for k in range(first_k, last_k, 4):
        row = [gram[k + e:k + e + 1, :] for e in range(4)]
        col = [gram[:, k + e:k + e + 1] for e in range(4)]
        block = [[wide(row[e][:, k + f:k + f + 1]) for f in range(4)] for e in range(4)]
        inside = (lane >= k) & (lane < k + 4)
        row = [jnp.where(lane == k + e, 1.0, jnp.where(inside, 0.0, row[e])) for e in range(4)]
        (a0, a1, b0, b1), (a2, a3, b2, b3), (c0, c1, d0, d1), (c2, c3, d2, d3) = block
        inv_a = 1.0 / (a0 * a3 - a1 * a2)
        x0, x1 = (a3 * b0 - a1 * b2) * inv_a, (a3 * b1 - a1 * b3) * inv_a
        x2, x3 = (a0 * b2 - a2 * b0) * inv_a, (a0 * b3 - a2 * b1) * inv_a
        s0, s1 = d0 - (c0 * x0 + c1 * x2), d1 - (c0 * x1 + c1 * x3)
        s2, s3 = d2 - (c2 * x0 + c3 * x2), d3 - (c2 * x1 + c3 * x3)
        inv_s = 1.0 / (s0 * s3 - s1 * s2)
        u0, u1 = (a3 * row[0] - a1 * row[1]) * inv_a, (a0 * row[1] - a2 * row[0]) * inv_a
        v0, v1 = row[2] - (c0 * u0 + c1 * u1), row[3] - (c2 * u0 + c3 * u1)
        new2, new3 = (s3 * v0 - s1 * v1) * inv_s, (s0 * v1 - s2 * v0) * inv_s
        new = [u0 - (x0 * new2 + x1 * new3), u1 - (x2 * new2 + x3 * new3), new2, new3]
        rest = jnp.where((cols >= k) & (cols < k + 4), 0.0, gram)
        gram = rest - (col[0] * new[0] + col[1] * new[1]) - (col[2] * new[2] + col[3] * new[3])
        for e in range(4):
            gram = jnp.where(rows == k + e, new[e], gram)
    return gram


def kernel(n, m, cut, rc, x_hbm, starts, x, lout, rout,
           clean, lg, sbuf, precv, srecv, rg, tsend, tcore, tsum, grq, grsum, glq, glsum, glall,
           rcat, rwide, acc, inv_r,
           lz_s, lx_s, l_r, p_s, p_r, s_s, s_r, gq_s, gq_r, ga_s, ga_r, hq_s, hq_r, ht_s, ht_r, ha_s, ha_r,
           r_s, r_r, tc_s, tc_r, ty_s, ty_r, rc_s, rc_r, x_sem):
    c = lax.axis_index("chan")
    t = lax.axis_index("tm")
    rank = starts.shape[0]
    lc = starts.shape[1] - rc
    lk = lc // cut
    times = x.shape[1]
    width = times // 2
    half = n // 2
    z, pair = t // 2, t % 2
    other = z * 2 + 1 - pair
    ys = m // 2
    y, core = c // 2, c % 2
    twin = y * 2 + 1 - core

    def flip(s):
        value, bit = 0, 1
        while bit < half:
            value = value + bit * ((z // bit + s // bit) % 2)
            bit *= 2
        return value

    def side(own):
        return pair * own + (1 - pair) * (1 - own)

    def mine(q):
        return q * 2 + pair

    def theirs(q):
        return q * 2 + 1 - pair

    def peer_t(s):
        return lax.rem(t + s, n)

    def peer_c(s):
        return lax.rem(c + s, m)

    def peer_y(s):
        return lax.rem(y + s, ys)

    def copy_t(src, dst, ssem, rsem, j):
        return pltpu.make_async_remote_copy(src_ref=src, dst_ref=dst, send_sem=ssem, recv_sem=rsem,
                                            device_id=(c, j), device_id_type=MESH)

    def copy_c(src, dst, ssem, rsem, j):
        return pltpu.make_async_remote_copy(src_ref=src, dst_ref=dst, send_sem=ssem, recv_sem=rsem,
                                            device_id=(j, t), device_id_type=MESH)

    def loop(first, last, body):
        def step(s, carry):
            body(s)
            return carry
        lax.fori_loop(first, last, step, 0)

    def left_mine(g, k):
        return starts.at[:, pl.ds(k * lk, lk)] if g == 0 else lg.at[g, k, t]

    def left_z(g, k, q, slot):
        return copy_t(left_mine(g, k), lg.at[g, k, slot], lz_s.at[g, k, q], l_r.at[g, k, slot], mine(q))

    def left_x(g, k, q, slot, own=False):
        return copy_t(left_mine(g, k) if own else lg.at[g, k, mine(q)], lg.at[g, k, slot], lx_s.at[g, k, q], l_r.at[g, k, slot], other)

    def left_send(g, k):
        loop(1, half, lambda s: left_z(g, k, flip(s), t).start())
        left_x(g, k, z, t, True).start()

    def left_own(g, k):
        def body(s):
            q = flip(s)
            left_z(g, k, q, mine(q)).wait_recv()
            left_x(g, k, q, mine(q)).start()
        loop(1, half, body)

    def left_other(g, k):
        loop(0, half, lambda s: left_x(g, k, s, theirs(s)).wait_recv())

    def pair_copy(i, k, q):
        return copy_t(sbuf.at[i, k, 0, q], precv.at[i, k, q], p_s.at[i, k, q], p_r.at[i, k, q], other)

    def pair_send(i, k):
        loop(0, half, lambda s: pair_copy(i, k, flip(half - 1 - s)).start())

    def s_copy(i, k, q, slot):
        return copy_t(sbuf.at[i, k, 1, q], srecv.at[i, k, slot], s_s.at[i, k, q], s_r.at[i, k, slot], mine(q))

    def join(i, k, s):
        q = flip(half - 1 - s)
        pair_copy(i, k, q).wait_recv()
        sbuf[i, k, 1, q] += precv[i, k, q]
        if s < half - 1:
            s_copy(i, k, q, z).start()

    def gq_copy(i, j, slot):
        return copy_t(grq.at[i, t, c], grq.at[i, slot, c], gq_s.at[i, j], gq_r.at[i, slot], j)

    def ga_copy(i, j, slot):
        return copy_c(grsum.at[i, c], grsum.at[i, slot], ga_s.at[i, j], ga_r.at[i, slot], j)

    def hq_copy(i, j, slot):
        return copy_c(glq.at[i, c, j], glq.at[i, slot, j], hq_s.at[i, j], hq_r.at[i, slot], j)

    def ht_copy(i, j, slot):
        return copy_t(glsum.at[i, t], glsum.at[i, slot], ht_s.at[i, j], ht_r.at[i, slot], j)

    def ha_copy(i, j, slot):
        return copy_c(glall.at[i, c], glall.at[i, slot], ha_s.at[i, j], ha_r.at[i, slot], j)

    def right_copy(j, slot):
        return copy_c(starts.at[:, pl.ds(lc, rc)], rg.at[0, slot], r_s.at[j], r_r.at[slot], j)

    def tc_copy(i, q):
        return copy_c(tsend.at[i, q], tcore.at[i, q], tc_s.at[i, q], tc_r.at[i, q], twin)

    def ty_copy(i, q, to, slot):
        return copy_c(tsum.at[i, y, q], tsum.at[i, slot, q], ty_s.at[i, q, to], ty_r.at[i, q, slot],
                      to * 2 + core)

    def rc_copy(i, q, who):
        at = q * 2 + who
        return copy_c(rg.at[i, q * 2 + core], rg.at[i, at], rc_s.at[i, q], rc_r.at[i, q], twin)

    def x_copy(j):
        at = pl.ds(pl.multiple_of(j * lc, lc), lc)
        return pltpu.make_async_copy(x_hbm.at[at], x.at[at], x_sem.at[j])

    barrier = pltpu.get_barrier_semaphore()
    loop(1, n, lambda s: pl.semaphore_signal(barrier, inc=1, device_id=(c, peer_t(s)), device_id_type=MESH))
    loop(1, m, lambda s: pl.semaphore_signal(barrier, inc=1, device_id=(peer_c(s), t), device_id_type=MESH))

    pl.semaphore_wait(barrier, n + m - 2)

    left_send(0, 0)
    loop(1, m, lambda s: right_copy(peer_c(s), c).start())
    for k in range(1, cut):
        left_send(0, k)
    loop(0, half, lambda s: x_copy(mine(s)).start())
    loop(0, half, lambda s: x_copy(theirs(s)).start())
    for k in range(cut):
        lg[0, k, t] = starts[:, k * lk:(k + 1) * lk]
    rg[0, c] = starts[:, lc:]

    rows = lax.broadcasted_iota(jnp.int32, (rank, rank), 0)
    cols = lax.broadcasted_iota(jnp.int32, (rank, rank), 1)
    ridge = jnp.where(rows == cols, RIDGE, 0.0).astype(jnp.float32)

    def when(cond, body):
        pl.when(cond)(body)

    for i in range(ITERS):
        last = i == ITERS - 1

        def prepare(q, total):
            part = rg[i, q]
            both = stacked(part)
            high = both[:rank]
            low = both[rank:]
            at = pl.ds(pl.multiple_of(q * rc, rc), rc)
            rcat[:, at] = jnp.concatenate([high, high, low, low], axis=0).astype(jnp.bfloat16)
            rwide[at, :] = both.T.astype(jnp.bfloat16)
            term = outer_gram(part)
            return term if total is None else total + term

        total = None
        if i == 0:
            left_own(0, 0)
            loop(1, m, lambda s: right_copy(c, peer_c(s)).wait_recv())
            for q in range(m):
                total = prepare(q, total)
        else:
            for q in range(ys):
                total = prepare(q * 2 + core, total)
            for q in range(ys):
                rc_copy(i, q, 1 - core).wait_recv()
                total = prepare(q * 2 + 1 - core, total)
        grq[i, t] = packed(total).reshape(m, rank // 2 // m, 2 * rank)
        loop(1, n, lambda s: gq_copy(i, peer_t(s), t).start())

        def share():
            loop(1, n, lambda s: gq_copy(i, t, peer_t(s)).wait_recv())
            value = grq[i, 0, c]
            for q in range(1, n):
                value = value + grq[i, q, c]
            grsum[i, c] = value
            loop(1, m, lambda s: ga_copy(i, peer_c(s), c).start())

        def block_a(k, own):
            js = [q * 2 + side(own) for q in range(half)]
            ats = [pl.ds(pl.multiple_of(j * lc + k * lk, lk), lk) for j in js]
            twos = [stacked(lg[i, k, j]).T.astype(jnp.bfloat16) for j in js]
            lcat = jnp.concatenate(twos, axis=0)
            lcat = jnp.concatenate([lcat, lcat], axis=1)
            deep = half * lk
            sums = None
            for b in range(times // width):
                part = pl.ds(b * width, width)
                values = jnp.concatenate([x[at, part] for at in ats], axis=0)
                low_rank = dot(lcat, rcat[:, part])
                residue = values - low_rank
                kept = jnp.clip(residue, -LEVEL, LEVEL)
                if last:
                    outlier = residue - kept
                    for q, at in enumerate(ats):
                        x[at, part] = outlier[q * lk:(q + 1) * lk]
                high, low = split(low_rank + kept)
                clean[0, k, own, :, part] = high
                clean[1, k, own, :, part] = low
                term = dot(jnp.concatenate([high, low], axis=0), rwide[part, :])
                sums = term if sums is None else sums + term
            flat = (sums[:deep] + sums[deep:]).T
            flat = flat[:rank] + flat[rank:]
            for q in range(half):
                sbuf[i, k, own, q] = flat[:, q * lk:(q + 1) * lk]

        if i == 0:
            def step_a(s, carry):
                k, own = s % cut, 1 - s // cut
                when((own == 1) & (k > 0), lambda: left_own(0, k))
                when(own == 0, lambda: left_other(0, k))
                when(k == 0, lambda: loop(0, half, lambda q: x_copy(q * 2 + side(own)).wait()))
                block_a(k, own)
                when(own == 0, lambda: pair_send(0, k))
                when((own == 1) & (k == cut - 1), share)
                return carry
            lax.fori_loop(0, 2 * cut, step_a, 0)
            joins = [(k, s) for k in range(cut) for s in range(half)]
        else:
            early = half // 2

            def step_a(s, carry):
                k, own = s % cut, s // cut
                block_a(k, own)
                when(own == 0, lambda: pair_send(i, k))

                @pl.when((own == 1) & (k == 0))
                def _():
                    share()
                    for j in range(early):
                        join(i, 0, j)
                return carry
            lax.fori_loop(0, 2 * cut, step_a, 0)
            joins = [(k, s) for k in range(cut) for s in range(half) if (k, s) >= (0, early)]

        free = 0
        while free < len(joins) and joins[free][0] == 0 and i > 0:
            join(i, *joins[free])
            free += 1
        joins = joins[free:]
        loop(1, m, lambda s: ga_copy(i, c, peer_c(s)).wait_recv())
        gram = unpacked(grsum[i].reshape(rank // 2, 2 * rank)) + ridge
        per = max(4, rank // (len(joins) + 1) // 4 * 4)
        done = 0
        for k, s in joins:
            gram = pivots(gram, done, min(done + per, rank))
            done = min(done + per, rank)
            join(i, k, s)
        inv_r[...] = pivots(gram, done, rank)

        for k in range(cut):
            def add_s(s, value):
                q = flip(s)
                s_copy(i, k, z, q).wait_recv()
                return value + srecv[i, k, q]

            total = lax.fori_loop(1, half, add_s, sbuf[i, k, 1, z])
            piece = solved(inv_r[...], total)
            lg[i + 1, k, t] = piece
            left_send(i + 1, k)
            term = outer_gram(piece)
            gram = term if k == 0 else gram + term
            if last:
                lout[:, k * lk:(k + 1) * lk] = piece

        glq[i, c] = packed(gram).reshape(m, rank // 2 // m, 2 * rank)
        loop(1, m, lambda s: hq_copy(i, peer_c(s), c).start())
        acc[...] = jnp.zeros_like(acc)

        def share_chan():
            loop(1, m, lambda s: hq_copy(i, c, peer_c(s)).wait_recv())
            value = glq[i, 0, c]
            for q in range(1, m):
                value = value + glq[i, q, c]
            glsum[i, t] = value
            loop(1, n, lambda s: ht_copy(i, peer_t(s), t).start())

        def share_tm():
            loop(1, n, lambda s: ht_copy(i, t, peer_t(s)).wait_recv())
            value = glsum[i, 0]
            for q in range(1, n):
                value = value + glsum[i, q]
            glall[i, c] = value
            loop(1, m, lambda s: ha_copy(i, peer_c(s), c).start())

        def step_b(s, carry):
            k, own = s % cut, 1 - s // cut
            when(own == 1, lambda: left_own(i + 1, k))
            when(own == 0, lambda: left_other(i + 1, k))
            value = jnp.concatenate([lg[i + 1, k, q * 2 + side(own)] for q in range(half)], axis=1)
            both = stacked(value).astype(jnp.bfloat16)
            for b in range(times // width):
                part = pl.ds(b * width, width)
                acc[:, part] += dot(both, clean[0, k, own, :, part]) + dot(both, clean[1, k, own, :, part])
            when(s == 0, share_chan)
            when(s == cut, share_tm)
            return carry
        lax.fori_loop(0, 2 * cut, step_b, 0)

        def t_part(q, who):
            at = pl.ds(pl.multiple_of((q * 2 + who) * rc, rc), rc)
            return acc[:rank, at] + acc[rank:, at]

        def t_send(q):
            tsend[i, q] = t_part(q, 1 - core)
            tc_copy(i, q).start()

        def t_join(q):
            tsum[i, y, q] = t_part(q, core)
            tc_copy(i, q).wait_recv()
            tsum[i, y, q] += tcore[i, q]

        def over_y(s):
            q = peer_y(s)
            t_join(q)
            if last:
                when(s < ys, lambda: ty_copy(i, q, q, y).start())
            else:
                loop(1, ys, lambda v: ty_copy(i, q, peer_y(v), y).start())

        loop(1, ys + 1, lambda s: t_send(peer_y(s)))
        loop(1, ys + 1, over_y)

        loop(1, m, lambda s: ha_copy(i, c, peer_c(s)).wait_recv())
        inv_l = pivots(unpacked(glall[i].reshape(rank // 2, 2 * rank)) + ridge, 0, rank)

        def total_of(q):
            value = tsum[i, 0, q]
            for v in range(1, ys):
                value = value + tsum[i, v, q]
            return value

        if last:
            loop(1, ys, lambda s: ty_copy(i, y, y, peer_y(s)).wait_recv())
            rout[...] = solved(inv_l, total_of(y))
        else:
            for q in range(ys):
                loop(1, ys, lambda s: ty_copy(i, q, y, peer_y(s)).wait_recv())
                rg[i + 1, q * 2 + core] = solved(inv_l, total_of(q))
                rc_copy(i + 1, q, core).start()

    loop(1, m, lambda s: right_copy(peer_c(s), c).wait_send())
    for i in range(ITERS):
        for k in range(cut):
            loop(0, half, lambda s: pair_copy(i, k, s).wait_send())
            loop(1, half, lambda s: s_copy(i, k, flip(s), z).wait_send())
        loop(1, n, lambda s: gq_copy(i, peer_t(s), t).wait_send())
        loop(1, m, lambda s: ga_copy(i, peer_c(s), c).wait_send())
        loop(1, m, lambda s: hq_copy(i, peer_c(s), c).wait_send())
        loop(1, n, lambda s: ht_copy(i, peer_t(s), t).wait_send())
        loop(1, m, lambda s: ha_copy(i, peer_c(s), c).wait_send())
        loop(0, ys, lambda q: tc_copy(i, q).wait_send())
        if i == ITERS - 1:
            loop(1, ys, lambda s: ty_copy(i, peer_y(s), peer_y(s), y).wait_send())
        else:
            for q in range(ys):
                loop(1, ys, lambda s: ty_copy(i, q, peer_y(s), y).wait_send())
            loop(0, ys, lambda q: rc_copy(i + 1, q, core).wait_send())
    for g in range(ITERS + 1):
        for k in range(cut):
            loop(1, half, lambda s: left_z(g, k, flip(s), t).wait_send())
            loop(0, half, lambda s: left_x(g, k, s, t).wait_send())


def store(parts, x, left, right, x_out, left_out, right_out, sem):
    rows = x.shape[0] // parts
    copies = [pltpu.make_async_copy(left, left_out, sem.at[parts]),
              pltpu.make_async_copy(right, right_out, sem.at[parts + 1])]
    for q in range(parts):
        at = pl.ds(q * rows, rows)
        copies.append(pltpu.make_async_copy(x.at[at], x_out.at[at], sem.at[q]))
    for copy in copies:
        copy.start()
    for copy in copies:
        copy.wait()


def shards(n, m, readings, channel_start, time_start):
    lc, rank = channel_start.shape
    rc = time_start.shape[0]
    rows, times = readings.shape
    cut = max(1, lc // LANES)
    lk, half, ys = lc // cut, n // 2, m // 2
    f32 = jnp.float32
    vmem = pl.BlockSpec(memory_space=pltpu.VMEM)
    hbm = pl.BlockSpec(memory_space=pltpu.HBM)
    dma = pltpu.SemaphoreType.DMA
    outliers, left, right = pl.pallas_call(
        functools.partial(kernel, n, m, cut, rc),
        out_shape=(jax.ShapeDtypeStruct((rows, times), f32),
                   jax.ShapeDtypeStruct((rank, lc), f32),
                   jax.ShapeDtypeStruct((rank, rc), f32)),
        in_specs=[hbm, vmem],
        out_specs=(vmem, vmem, vmem),
        scratch_shapes=[
            pltpu.VMEM((2, cut, 2, half * lk, times), jnp.bfloat16),
            pltpu.VMEM((ITERS + 1, cut, n, rank, lk), f32),
            pltpu.VMEM((ITERS, cut, 2, half, rank, lk), f32),
            pltpu.VMEM((ITERS, cut, half, rank, lk), f32),
            pltpu.VMEM((ITERS, cut, half, rank, lk), f32),
            pltpu.VMEM((ITERS, m, rank, rc), f32),
            pltpu.VMEM((ITERS, ys, rank, rc), f32),
            pltpu.VMEM((ITERS, ys, rank, rc), f32),
            pltpu.VMEM((ITERS, ys, ys, rank, rc), f32),
            pltpu.VMEM((ITERS, n, m, rank // 2 // m, 2 * rank), f32),
            pltpu.VMEM((ITERS, m, rank // 2 // m, 2 * rank), f32),
            pltpu.VMEM((ITERS, m, m, rank // 2 // m, 2 * rank), f32),
            pltpu.VMEM((ITERS, n, rank // 2 // m, 2 * rank), f32),
            pltpu.VMEM((ITERS, m, rank // 2 // m, 2 * rank), f32),
            pltpu.VMEM((4 * rank, times), jnp.bfloat16),
            pltpu.VMEM((times, 2 * rank), jnp.bfloat16),
            pltpu.VMEM((2 * rank, times), f32),
            pltpu.VMEM((rank, rank), f32),
            dma((ITERS + 1, cut, half)), dma((ITERS + 1, cut, half)), dma((ITERS + 1, cut, n)),
            dma((ITERS, cut, half)), dma((ITERS, cut, half)),
            dma((ITERS, cut, half)), dma((ITERS, cut, half)),
            dma((ITERS, n)), dma((ITERS, n)),
            dma((ITERS, m)), dma((ITERS, m)),
            dma((ITERS, m)), dma((ITERS, m)),
            dma((ITERS, n)), dma((ITERS, n)),
            dma((ITERS, m)), dma((ITERS, m)),
            dma((m,)), dma((m,)),
            dma((ITERS, ys)), dma((ITERS, ys)),
            dma((ITERS, ys, ys)), dma((ITERS, ys, ys)),
            dma((ITERS, ys)), dma((ITERS, ys)),
            dma((n,)),
        ],
        compiler_params=pltpu.CompilerParams(collective_id=0, has_side_effects=True,
                                             vmem_limit_bytes=42 * 1024 * 1024),
    )(readings, jnp.concatenate([channel_start.T, time_start.T], axis=1))
    parts = 8
    outliers, left, right = pl.pallas_call(
        functools.partial(store, parts),
        out_shape=(jax.ShapeDtypeStruct((rows, times), f32),
                   jax.ShapeDtypeStruct((rank, lc), f32),
                   jax.ShapeDtypeStruct((rank, rc), f32)),
        in_specs=[pl.BlockSpec(memory_space=pl.ANY)] * 3,
        out_specs=(hbm, hbm, hbm),
        scratch_shapes=[dma((parts + 2,))],
        compiler_params=pltpu.CompilerParams(vmem_limit_bytes=4 * 1024 * 1024),
    )(outliers, left, right)
    return outliers, left.T, right.T


def solution(mesh):
    n, m = mesh.shape["tm"], mesh.shape["chan"]
    specs = (P("chan", "tm"), P(("chan", "tm"), None), P(("tm", "chan"), None))
    return jax.shard_map(functools.partial(shards, n, m), mesh=mesh, in_specs=specs, out_specs=specs,
                         check_vma=False)
```

```python
import functools

import jax
import jax.numpy as jnp
from jax import lax
from jax.experimental import pallas as pl
from jax.experimental.pallas import tpu as pltpu
from jax.sharding import PartitionSpec as P

ITERS = 2
LEVEL = 1.5
RIDGE = 8.0
LANES = 128
MESH = pl.DeviceIdType.MESH
HIGHEST = lax.Precision.HIGHEST


def split(value):
    high = value.astype(jnp.bfloat16)
    low = (value - high.astype(jnp.float32)).astype(jnp.bfloat16)
    return high, low


def stacked(value):
    high = value.astype(jnp.bfloat16).astype(jnp.float32)
    return jnp.concatenate([high, value - high], axis=0)


def dot(first, second):
    return jnp.dot(first, second, preferred_element_type=jnp.float32)


def solved(inv, value):
    return jnp.dot(inv, value, precision=HIGHEST, preferred_element_type=jnp.float32)


def outer_gram(value):
    return lax.dot_general(value, value, (((1,), (1,)), ((), ())), precision=HIGHEST,
                           preferred_element_type=jnp.float32)


def packed(gram):
    half = gram.shape[0] // 2
    return jnp.concatenate([gram[:half], gram[half:]], axis=1)


def unpacked(value):
    rank = value.shape[0] * 2
    return jnp.concatenate([value[:, :rank], value[:, rank:]], axis=0)


def pivots(gram, first_k, last_k):
    rank = gram.shape[0]
    rows = lax.broadcasted_iota(jnp.int32, (rank, rank), 0)
    cols = lax.broadcasted_iota(jnp.int32, (rank, rank), 1)
    lane = cols[:1]
    wide = lambda value: jnp.broadcast_to(value, (1, rank))
    for k in range(first_k, last_k, 4):
        row = [gram[k + e:k + e + 1, :] for e in range(4)]
        col = [gram[:, k + e:k + e + 1] for e in range(4)]
        block = [[wide(row[e][:, k + f:k + f + 1]) for f in range(4)] for e in range(4)]
        inside = (lane >= k) & (lane < k + 4)
        row = [jnp.where(lane == k + e, 1.0, jnp.where(inside, 0.0, row[e])) for e in range(4)]
        (a0, a1, b0, b1), (a2, a3, b2, b3), (c0, c1, d0, d1), (c2, c3, d2, d3) = block
        inv_a = 1.0 / (a0 * a3 - a1 * a2)
        x0, x1 = (a3 * b0 - a1 * b2) * inv_a, (a3 * b1 - a1 * b3) * inv_a
        x2, x3 = (a0 * b2 - a2 * b0) * inv_a, (a0 * b3 - a2 * b1) * inv_a
        s0, s1 = d0 - (c0 * x0 + c1 * x2), d1 - (c0 * x1 + c1 * x3)
        s2, s3 = d2 - (c2 * x0 + c3 * x2), d3 - (c2 * x1 + c3 * x3)
        inv_s = 1.0 / (s0 * s3 - s1 * s2)
        u0, u1 = (a3 * row[0] - a1 * row[1]) * inv_a, (a0 * row[1] - a2 * row[0]) * inv_a
        v0, v1 = row[2] - (c0 * u0 + c1 * u1), row[3] - (c2 * u0 + c3 * u1)
        new2, new3 = (s3 * v0 - s1 * v1) * inv_s, (s0 * v1 - s2 * v0) * inv_s
        new = [u0 - (x0 * new2 + x1 * new3), u1 - (x2 * new2 + x3 * new3), new2, new3]
        rest = jnp.where((cols >= k) & (cols < k + 4), 0.0, gram)
        gram = rest - (col[0] * new[0] + col[1] * new[1]) - (col[2] * new[2] + col[3] * new[3])
        for e in range(4):
            gram = jnp.where(rows == k + e, new[e], gram)
    return gram


def kernel(n, m, cut, rc, x_hbm, starts, x, lout, rout,
           clean, lg, sbuf, precv, srecv, rg, tsend, tcore, tsum, grq, grsum, glq, glsum, glall,
           rcat, rwide, acc, inv_r,
           lz_s, lx_s, l_r, p_s, p_r, s_s, s_r, gq_s, gq_r, ga_s, ga_r, hq_s, hq_r, ht_s, ht_r, ha_s, ha_r,
           r_s, r_r, tc_s, tc_r, ty_s, ty_r, rc_s, rc_r, x_sem):
    c = lax.axis_index("chan")
    t = lax.axis_index("tm")
    rank = starts.shape[0]
    lc = starts.shape[1] - rc
    lk = lc // cut
    times = x.shape[1]
    width = times // 2
    half = n // 2
    z, pair = t // 2, t % 2
    other = z * 2 + 1 - pair
    ys = m // 2
    y, core = c // 2, c % 2
    twin = y * 2 + 1 - core

    def flip(s):
        value, bit = 0, 1
        while bit < half:
            value = value + bit * ((z // bit + s // bit) % 2)
            bit *= 2
        return value

    def side(own):
        return pair * own + (1 - pair) * (1 - own)

    def mine(q):
        return q * 2 + pair

    def theirs(q):
        return q * 2 + 1 - pair

    def peer_t(s):
        return lax.rem(t + s, n)

    def peer_c(s):
        return lax.rem(c + s, m)

    def peer_y(s):
        return lax.rem(y + s, ys)

    def copy_t(src, dst, ssem, rsem, j):
        return pltpu.make_async_remote_copy(src_ref=src, dst_ref=dst, send_sem=ssem, recv_sem=rsem,
                                            device_id=(c, j), device_id_type=MESH)

    def copy_c(src, dst, ssem, rsem, j):
        return pltpu.make_async_remote_copy(src_ref=src, dst_ref=dst, send_sem=ssem, recv_sem=rsem,
                                            device_id=(j, t), device_id_type=MESH)

    def loop(first, last, body):
        def step(s, carry):
            body(s)
            return carry
        lax.fori_loop(first, last, step, 0)

    def left_mine(g, k):
        return starts.at[:, pl.ds(k * lk, lk)] if g == 0 else lg.at[g, k, t]

    def left_z(g, k, q, slot):
        return copy_t(left_mine(g, k), lg.at[g, k, slot], lz_s.at[g, k, q], l_r.at[g, k, slot], mine(q))

    def left_x(g, k, q, slot, own=False):
        return copy_t(left_mine(g, k) if own else lg.at[g, k, mine(q)], lg.at[g, k, slot], lx_s.at[g, k, q], l_r.at[g, k, slot], other)

    def left_send(g, k):
        loop(1, half, lambda s: left_z(g, k, flip(s), t).start())
        left_x(g, k, z, t, True).start()

    def left_own(g, k):
        def body(s):
            q = flip(s)
            left_z(g, k, q, mine(q)).wait_recv()
            left_x(g, k, q, mine(q)).start()
        loop(1, half, body)

    def left_other(g, k):
        loop(0, half, lambda s: left_x(g, k, s, theirs(s)).wait_recv())

    def pair_copy(i, k, q):
        return copy_t(sbuf.at[i, k, 0, q], precv.at[i, k, q], p_s.at[i, k, q], p_r.at[i, k, q], other)

    def pair_send(i, k):
        loop(0, half, lambda s: pair_copy(i, k, flip(half - 1 - s)).start())

    def s_copy(i, k, q, slot):
        return copy_t(sbuf.at[i, k, 1, q], srecv.at[i, k, slot], s_s.at[i, k, q], s_r.at[i, k, slot], mine(q))

    def join(i, k, s):
        q = flip(half - 1 - s)
        pair_copy(i, k, q).wait_recv()
        sbuf[i, k, 1, q] += precv[i, k, q]
        if s < half - 1:
            s_copy(i, k, q, z).start()

    def gq_copy(i, j, slot):
        return copy_t(grq.at[i, t, c], grq.at[i, slot, c], gq_s.at[i, j], gq_r.at[i, slot], j)

    def ga_copy(i, j, slot):
        return copy_c(grsum.at[i, c], grsum.at[i, slot], ga_s.at[i, j], ga_r.at[i, slot], j)

    def hq_copy(i, j, slot):
        return copy_c(glq.at[i, c, j], glq.at[i, slot, j], hq_s.at[i, j], hq_r.at[i, slot], j)

    def ht_copy(i, j, slot):
        return copy_t(glsum.at[i, t], glsum.at[i, slot], ht_s.at[i, j], ht_r.at[i, slot], j)

    def ha_copy(i, j, slot):
        return copy_c(glall.at[i, c], glall.at[i, slot], ha_s.at[i, j], ha_r.at[i, slot], j)

    def right_copy(j, slot):
        return copy_c(starts.at[:, pl.ds(lc, rc)], rg.at[0, slot], r_s.at[j], r_r.at[slot], j)

    def tc_copy(i, q):
        return copy_c(tsend.at[i, q], tcore.at[i, q], tc_s.at[i, q], tc_r.at[i, q], twin)

    def ty_copy(i, q, to, slot):
        return copy_c(tsum.at[i, y, q], tsum.at[i, slot, q], ty_s.at[i, q, to], ty_r.at[i, q, slot],
                      to * 2 + core)

    def rc_copy(i, q, who):
        at = q * 2 + who
        return copy_c(rg.at[i, q * 2 + core], rg.at[i, at], rc_s.at[i, q], rc_r.at[i, q], twin)

    def x_copy(j):
        at = pl.ds(pl.multiple_of(j * lc, lc), lc)
        return pltpu.make_async_copy(x_hbm.at[at], x.at[at], x_sem.at[j])

    barrier = pltpu.get_barrier_semaphore()
    loop(1, n, lambda s: pl.semaphore_signal(barrier, inc=1, device_id=(c, peer_t(s)), device_id_type=MESH))
    loop(1, m, lambda s: pl.semaphore_signal(barrier, inc=1, device_id=(peer_c(s), t), device_id_type=MESH))

    pl.semaphore_wait(barrier, n + m - 2)

    left_send(0, 0)
    loop(1, m, lambda s: right_copy(peer_c(s), c).start())
    for k in range(1, cut):
        left_send(0, k)
    loop(0, half, lambda s: x_copy(mine(s)).start())
    loop(0, half, lambda s: x_copy(theirs(s)).start())
    for k in range(cut):
        lg[0, k, t] = starts[:, k * lk:(k + 1) * lk]
    rg[0, c] = starts[:, lc:]

    rows = lax.broadcasted_iota(jnp.int32, (rank, rank), 0)
    cols = lax.broadcasted_iota(jnp.int32, (rank, rank), 1)
    ridge = jnp.where(rows == cols, RIDGE, 0.0).astype(jnp.float32)

    def when(cond, body):
        pl.when(cond)(body)

    for i in range(ITERS):
        last = i == ITERS - 1

        def prepare(q, total):
            part = rg[i, q]
            both = stacked(part)
            high = both[:rank]
            low = both[rank:]
            at = pl.ds(pl.multiple_of(q * rc, rc), rc)
            rcat[:, at] = jnp.concatenate([high, high, low, low], axis=0).astype(jnp.bfloat16)
            rwide[at, :] = both.T.astype(jnp.bfloat16)
            term = outer_gram(part)
            return term if total is None else total + term

        total = None
        if i == 0:
            left_own(0, 0)
            loop(1, m, lambda s: right_copy(c, peer_c(s)).wait_recv())
            for q in range(m):
                total = prepare(q, total)
        else:
            for q in range(ys):
                total = prepare(q * 2 + core, total)
            for q in range(ys):
                rc_copy(i, q, 1 - core).wait_recv()
                total = prepare(q * 2 + 1 - core, total)
        grq[i, t] = packed(total).reshape(m, rank // 2 // m, 2 * rank)
        loop(1, n, lambda s: gq_copy(i, peer_t(s), t).start())

        def share():
            loop(1, n, lambda s: gq_copy(i, t, peer_t(s)).wait_recv())
            value = grq[i, 0, c]
            for q in range(1, n):
                value = value + grq[i, q, c]
            grsum[i, c] = value
            loop(1, m, lambda s: ga_copy(i, peer_c(s), c).start())

        def block_a(k, own):
            js = [q * 2 + side(own) for q in range(half)]
            ats = [pl.ds(pl.multiple_of(j * lc + k * lk, lk), lk) for j in js]
            twos = [stacked(lg[i, k, j]).T.astype(jnp.bfloat16) for j in js]
            lcat = jnp.concatenate(twos, axis=0)
            lcat = jnp.concatenate([lcat, lcat], axis=1)
            deep = half * lk
            sums = None
            for b in range(times // width):
                part = pl.ds(b * width, width)
                values = jnp.concatenate([x[at, part] for at in ats], axis=0)
                low_rank = dot(lcat, rcat[:, part])
                residue = values - low_rank
                kept = jnp.clip(residue, -LEVEL, LEVEL)
                if last:
                    outlier = residue - kept
                    for q, at in enumerate(ats):
                        x[at, part] = outlier[q * lk:(q + 1) * lk]
                high, low = split(low_rank + kept)
                clean[0, k, own, :, part] = high
                clean[1, k, own, :, part] = low
                term = dot(jnp.concatenate([high, low], axis=0), rwide[part, :])
                sums = term if sums is None else sums + term
            flat = (sums[:deep] + sums[deep:]).T
            flat = flat[:rank] + flat[rank:]
            for q in range(half):
                sbuf[i, k, own, q] = flat[:, q * lk:(q + 1) * lk]

        if i == 0:
            def step_a(s, carry):
                k, own = s // 2, 1 - s % 2
                when((own == 0) & (k < cut - 1), lambda: left_own(0, k + 1))
                when(own == 0, lambda: left_other(0, k))
                when(k == 0, lambda: loop(0, half, lambda q: x_copy(q * 2 + side(own)).wait()))
                block_a(k, own)
                when(own == 0, lambda: pair_send(0, k))
                when((own == 1) & (k == cut - 1), share)
                return carry
            lax.fori_loop(0, 2 * cut, step_a, 0)
            joins = [(k, s) for k in range(cut) for s in range(half)]
        else:
            early = half // 2

            def step_a(s, carry):
                k, own = s % cut, s // cut
                block_a(k, own)
                when(own == 0, lambda: pair_send(i, k))

                @pl.when((own == 1) & (k == 0))
                def _():
                    share()
                    for j in range(early):
                        join(i, 0, j)
                return carry
            lax.fori_loop(0, 2 * cut, step_a, 0)
            joins = [(k, s) for k in range(cut) for s in range(half) if (k, s) >= (0, early)]

        free = 0
        while free < len(joins) and joins[free][0] == 0 and i > 0:
            join(i, *joins[free])
            free += 1
        joins = joins[free:]
        loop(1, m, lambda s: ga_copy(i, c, peer_c(s)).wait_recv())
        gram = unpacked(grsum[i].reshape(rank // 2, 2 * rank)) + ridge
        per = max(4, rank // (len(joins) + 1) // 4 * 4)
        done = 0
        for k, s in joins:
            gram = pivots(gram, done, min(done + per, rank))
            done = min(done + per, rank)
            join(i, k, s)
        inv_r[...] = pivots(gram, done, rank)

        for k in range(cut):
            def add_s(s, value):
                q = flip(s)
                s_copy(i, k, z, q).wait_recv()
                return value + srecv[i, k, q]

            total = lax.fori_loop(1, half, add_s, sbuf[i, k, 1, z])
            piece = solved(inv_r[...], total)
            lg[i + 1, k, t] = piece
            left_send(i + 1, k)
            term = outer_gram(piece)
            gram = term if k == 0 else gram + term
            if last:
                lout[:, k * lk:(k + 1) * lk] = piece

        glq[i, c] = packed(gram).reshape(m, rank // 2 // m, 2 * rank)
        loop(1, m, lambda s: hq_copy(i, peer_c(s), c).start())
        acc[...] = jnp.zeros_like(acc)

        def share_chan():
            loop(1, m, lambda s: hq_copy(i, c, peer_c(s)).wait_recv())
            value = glq[i, 0, c]
            for q in range(1, m):
                value = value + glq[i, q, c]
            glsum[i, t] = value
            loop(1, n, lambda s: ht_copy(i, peer_t(s), t).start())

        def share_tm():
            loop(1, n, lambda s: ht_copy(i, t, peer_t(s)).wait_recv())
            value = glsum[i, 0]
            for q in range(1, n):
                value = value + glsum[i, q]
            glall[i, c] = value
            loop(1, m, lambda s: ha_copy(i, peer_c(s), c).start())

        def step_b(s, carry):
            k, own = s % cut, 1 - s // cut
            when(own == 1, lambda: left_own(i + 1, k))
            when(own == 0, lambda: left_other(i + 1, k))
            value = jnp.concatenate([lg[i + 1, k, q * 2 + side(own)] for q in range(half)], axis=1)
            both = stacked(value).astype(jnp.bfloat16)
            for b in range(times // width):
                part = pl.ds(b * width, width)
                acc[:, part] += dot(both, clean[0, k, own, :, part]) + dot(both, clean[1, k, own, :, part])
            when(s == 0, share_chan)
            when(s == cut, share_tm)
            return carry
        lax.fori_loop(0, 2 * cut, step_b, 0)

        def t_part(q, who):
            at = pl.ds(pl.multiple_of((q * 2 + who) * rc, rc), rc)
            return acc[:rank, at] + acc[rank:, at]

        def t_send(q):
            tsend[i, q] = t_part(q, 1 - core)
            tc_copy(i, q).start()

        def t_join(q):
            tsum[i, y, q] = t_part(q, core)
            tc_copy(i, q).wait_recv()
            tsum[i, y, q] += tcore[i, q]

        def over_y(s):
            q = peer_y(s)
            t_join(q)
            if last:
                when(s < ys, lambda: ty_copy(i, q, q, y).start())
            else:
                loop(1, ys, lambda v: ty_copy(i, q, peer_y(v), y).start())

        loop(1, ys + 1, lambda s: t_send(peer_y(s)))
        loop(1, ys + 1, over_y)

        loop(1, m, lambda s: ha_copy(i, c, peer_c(s)).wait_recv())
        inv_l = pivots(unpacked(glall[i].reshape(rank // 2, 2 * rank)) + ridge, 0, rank)

        def total_of(q):
            value = tsum[i, 0, q]
            for v in range(1, ys):
                value = value + tsum[i, v, q]
            return value

        if last:
            loop(1, ys, lambda s: ty_copy(i, y, y, peer_y(s)).wait_recv())
            rout[...] = solved(inv_l, total_of(y))
        else:
            for q in range(ys):
                loop(1, ys, lambda s: ty_copy(i, q, y, peer_y(s)).wait_recv())
                rg[i + 1, q * 2 + core] = solved(inv_l, total_of(q))
                rc_copy(i + 1, q, core).start()

    loop(1, m, lambda s: right_copy(peer_c(s), c).wait_send())
    for i in range(ITERS):
        for k in range(cut):
            loop(0, half, lambda s: pair_copy(i, k, s).wait_send())
            loop(1, half, lambda s: s_copy(i, k, flip(s), z).wait_send())
        loop(1, n, lambda s: gq_copy(i, peer_t(s), t).wait_send())
        loop(1, m, lambda s: ga_copy(i, peer_c(s), c).wait_send())
        loop(1, m, lambda s: hq_copy(i, peer_c(s), c).wait_send())
        loop(1, n, lambda s: ht_copy(i, peer_t(s), t).wait_send())
        loop(1, m, lambda s: ha_copy(i, peer_c(s), c).wait_send())
        loop(0, ys, lambda q: tc_copy(i, q).wait_send())
        if i == ITERS - 1:
            loop(1, ys, lambda s: ty_copy(i, peer_y(s), peer_y(s), y).wait_send())
        else:
            for q in range(ys):
                loop(1, ys, lambda s: ty_copy(i, q, peer_y(s), y).wait_send())
            loop(0, ys, lambda q: rc_copy(i + 1, q, core).wait_send())
    for g in range(ITERS + 1):
        for k in range(cut):
            loop(1, half, lambda s: left_z(g, k, flip(s), t).wait_send())
            loop(0, half, lambda s: left_x(g, k, s, t).wait_send())


def store(parts, x, left, right, x_out, left_out, right_out, sem):
    rows = x.shape[0] // parts
    copies = [pltpu.make_async_copy(left, left_out, sem.at[parts]),
              pltpu.make_async_copy(right, right_out, sem.at[parts + 1])]
    for q in range(parts):
        at = pl.ds(q * rows, rows)
        copies.append(pltpu.make_async_copy(x.at[at], x_out.at[at], sem.at[q]))
    for copy in copies:
        copy.start()
    for copy in copies:
        copy.wait()


def shards(n, m, readings, channel_start, time_start):
    lc, rank = channel_start.shape
    rc = time_start.shape[0]
    rows, times = readings.shape
    cut = max(1, lc // LANES)
    lk, half, ys = lc // cut, n // 2, m // 2
    f32 = jnp.float32
    vmem = pl.BlockSpec(memory_space=pltpu.VMEM)
    hbm = pl.BlockSpec(memory_space=pltpu.HBM)
    dma = pltpu.SemaphoreType.DMA
    outliers, left, right = pl.pallas_call(
        functools.partial(kernel, n, m, cut, rc),
        out_shape=(jax.ShapeDtypeStruct((rows, times), f32),
                   jax.ShapeDtypeStruct((rank, lc), f32),
                   jax.ShapeDtypeStruct((rank, rc), f32)),
        in_specs=[hbm, vmem],
        out_specs=(vmem, vmem, vmem),
        scratch_shapes=[
            pltpu.VMEM((2, cut, 2, half * lk, times), jnp.bfloat16),
            pltpu.VMEM((ITERS + 1, cut, n, rank, lk), f32),
            pltpu.VMEM((ITERS, cut, 2, half, rank, lk), f32),
            pltpu.VMEM((ITERS, cut, half, rank, lk), f32),
            pltpu.VMEM((ITERS, cut, half, rank, lk), f32),
            pltpu.VMEM((ITERS, m, rank, rc), f32),
            pltpu.VMEM((ITERS, ys, rank, rc), f32),
            pltpu.VMEM((ITERS, ys, rank, rc), f32),
            pltpu.VMEM((ITERS, ys, ys, rank, rc), f32),
            pltpu.VMEM((ITERS, n, m, rank // 2 // m, 2 * rank), f32),
            pltpu.VMEM((ITERS, m, rank // 2 // m, 2 * rank), f32),
            pltpu.VMEM((ITERS, m, m, rank // 2 // m, 2 * rank), f32),
            pltpu.VMEM((ITERS, n, rank // 2 // m, 2 * rank), f32),
            pltpu.VMEM((ITERS, m, rank // 2 // m, 2 * rank), f32),
            pltpu.VMEM((4 * rank, times), jnp.bfloat16),
            pltpu.VMEM((times, 2 * rank), jnp.bfloat16),
            pltpu.VMEM((2 * rank, times), f32),
            pltpu.VMEM((rank, rank), f32),
            dma((ITERS + 1, cut, half)), dma((ITERS + 1, cut, half)), dma((ITERS + 1, cut, n)),
            dma((ITERS, cut, half)), dma((ITERS, cut, half)),
            dma((ITERS, cut, half)), dma((ITERS, cut, half)),
            dma((ITERS, n)), dma((ITERS, n)),
            dma((ITERS, m)), dma((ITERS, m)),
            dma((ITERS, m)), dma((ITERS, m)),
            dma((ITERS, n)), dma((ITERS, n)),
            dma((ITERS, m)), dma((ITERS, m)),
            dma((m,)), dma((m,)),
            dma((ITERS, ys)), dma((ITERS, ys)),
            dma((ITERS, ys, ys)), dma((ITERS, ys, ys)),
            dma((ITERS, ys)), dma((ITERS, ys)),
            dma((n,)),
        ],
        compiler_params=pltpu.CompilerParams(collective_id=0, has_side_effects=True,
                                             vmem_limit_bytes=42 * 1024 * 1024),
    )(readings, jnp.concatenate([channel_start.T, time_start.T], axis=1))
    parts = 8
    outliers, left, right = pl.pallas_call(
        functools.partial(store, parts),
        out_shape=(jax.ShapeDtypeStruct((rows, times), f32),
                   jax.ShapeDtypeStruct((rank, lc), f32),
                   jax.ShapeDtypeStruct((rank, rc), f32)),
        in_specs=[pl.BlockSpec(memory_space=pl.ANY)] * 3,
        out_specs=(hbm, hbm, hbm),
        scratch_shapes=[dma((parts + 2,))],
        compiler_params=pltpu.CompilerParams(vmem_limit_bytes=4 * 1024 * 1024),
    )(outliers, left, right)
    return outliers, left.T, right.T


def solution(mesh):
    n, m = mesh.shape["tm"], mesh.shape["chan"]
    specs = (P("chan", "tm"), P(("chan", "tm"), None), P(("tm", "chan"), None))
    return jax.shard_map(functools.partial(shards, n, m), mesh=mesh, in_specs=specs, out_specs=specs,
                         check_vma=False)
```

```python
import functools

import jax
import jax.numpy as jnp
from jax import lax
from jax.experimental import pallas as pl
from jax.experimental.pallas import tpu as pltpu
from jax.sharding import PartitionSpec as P

ITERS = 2
LEVEL = 1.5
RIDGE = 8.0
LANES = 128
MESH = pl.DeviceIdType.MESH
HIGHEST = lax.Precision.HIGHEST


def split(value):
    high = value.astype(jnp.bfloat16)
    low = (value - high.astype(jnp.float32)).astype(jnp.bfloat16)
    return high, low


def stacked(value):
    high = value.astype(jnp.bfloat16).astype(jnp.float32)
    return jnp.concatenate([high, value - high], axis=0)


def dot(first, second):
    return jnp.dot(first, second, preferred_element_type=jnp.float32)


def solved(inv, value):
    return jnp.dot(inv, value, precision=HIGHEST, preferred_element_type=jnp.float32)


def outer_gram(value):
    return lax.dot_general(value, value, (((1,), (1,)), ((), ())), precision=HIGHEST,
                           preferred_element_type=jnp.float32)


def packed(gram):
    half = gram.shape[0] // 2
    return jnp.concatenate([gram[:half], gram[half:]], axis=1)


def unpacked(value):
    rank = value.shape[0] * 2
    return jnp.concatenate([value[:, :rank], value[:, rank:]], axis=0)


def pivots(gram, first_k, last_k):
    rank = gram.shape[0]
    rows = lax.broadcasted_iota(jnp.int32, (rank, rank), 0)
    cols = lax.broadcasted_iota(jnp.int32, (rank, rank), 1)
    lane = cols[:1]
    wide = lambda value: jnp.broadcast_to(value, (1, rank))
    for k in range(first_k, last_k, 4):
        row = [gram[k + e:k + e + 1, :] for e in range(4)]
        col = [gram[:, k + e:k + e + 1] for e in range(4)]
        block = [[wide(row[e][:, k + f:k + f + 1]) for f in range(4)] for e in range(4)]
        inside = (lane >= k) & (lane < k + 4)
        row = [jnp.where(lane == k + e, 1.0, jnp.where(inside, 0.0, row[e])) for e in range(4)]
        (a0, a1, b0, b1), (a2, a3, b2, b3), (c0, c1, d0, d1), (c2, c3, d2, d3) = block
        inv_a = 1.0 / (a0 * a3 - a1 * a2)
        x0, x1 = (a3 * b0 - a1 * b2) * inv_a, (a3 * b1 - a1 * b3) * inv_a
        x2, x3 = (a0 * b2 - a2 * b0) * inv_a, (a0 * b3 - a2 * b1) * inv_a
        s0, s1 = d0 - (c0 * x0 + c1 * x2), d1 - (c0 * x1 + c1 * x3)
        s2, s3 = d2 - (c2 * x0 + c3 * x2), d3 - (c2 * x1 + c3 * x3)
        inv_s = 1.0 / (s0 * s3 - s1 * s2)
        u0, u1 = (a3 * row[0] - a1 * row[1]) * inv_a, (a0 * row[1] - a2 * row[0]) * inv_a
        v0, v1 = row[2] - (c0 * u0 + c1 * u1), row[3] - (c2 * u0 + c3 * u1)
        new2, new3 = (s3 * v0 - s1 * v1) * inv_s, (s0 * v1 - s2 * v0) * inv_s
        new = [u0 - (x0 * new2 + x1 * new3), u1 - (x2 * new2 + x3 * new3), new2, new3]
        rest = jnp.where((cols >= k) & (cols < k + 4), 0.0, gram)
        gram = rest - (col[0] * new[0] + col[1] * new[1]) - (col[2] * new[2] + col[3] * new[3])
        for e in range(4):
            gram = jnp.where(rows == k + e, new[e], gram)
    return gram


def kernel(n, m, cut, rc, x_hbm, starts, x, lout, rout,
           clean, lg, sbuf, precv, srecv, rg, tsend, tcore, tsum, grq, grsum, glq, glsum, glall,
           rcat, rwide, acc, inv_r,
           lz_s, lx_s, l_r, p_s, p_r, s_s, s_r, gq_s, gq_r, ga_s, ga_r, hq_s, hq_r, ht_s, ht_r, ha_s, ha_r,
           r_s, r_r, tc_s, tc_r, ty_s, ty_r, rc_s, rc_r, x_sem):
    c = lax.axis_index("chan")
    t = lax.axis_index("tm")
    rank = starts.shape[0]
    lc = starts.shape[1] - rc
    lk = lc // cut
    times = x.shape[1]
    width = times // 2
    half = n // 2
    z, pair = t // 2, t % 2
    other = z * 2 + 1 - pair
    ys = m // 2
    y, core = c // 2, c % 2
    twin = y * 2 + 1 - core

    def flip(s):
        value, bit = 0, 1
        while bit < half:
            value = value + bit * ((z // bit + s // bit) % 2)
            bit *= 2
        return value

    def side(own):
        return pair * own + (1 - pair) * (1 - own)

    def mine(q):
        return q * 2 + pair

    def theirs(q):
        return q * 2 + 1 - pair

    def peer_t(s):
        return lax.rem(t + s, n)

    def peer_c(s):
        return lax.rem(c + s, m)

    def peer_y(s):
        return lax.rem(y + s, ys)

    def copy_t(src, dst, ssem, rsem, j):
        return pltpu.make_async_remote_copy(src_ref=src, dst_ref=dst, send_sem=ssem, recv_sem=rsem,
                                            device_id=(c, j), device_id_type=MESH)

    def copy_c(src, dst, ssem, rsem, j):
        return pltpu.make_async_remote_copy(src_ref=src, dst_ref=dst, send_sem=ssem, recv_sem=rsem,
                                            device_id=(j, t), device_id_type=MESH)

    def loop(first, last, body):
        def step(s, carry):
            body(s)
            return carry
        lax.fori_loop(first, last, step, 0)

    def left_mine(g, k):
        return starts.at[:, pl.ds(k * lk, lk)] if g == 0 else lg.at[g, k, t]

    def left_z(g, k, q, slot):
        return copy_t(left_mine(g, k), lg.at[g, k, slot], lz_s.at[g, k, q], l_r.at[g, k, slot], mine(q))

    def left_x(g, k, q, slot, own=False):
        return copy_t(left_mine(g, k) if own else lg.at[g, k, mine(q)], lg.at[g, k, slot], lx_s.at[g, k, q], l_r.at[g, k, slot], other)

    def left_send(g, k):
        loop(1, half, lambda s: left_z(g, k, flip(s), t).start())
        left_x(g, k, z, t, True).start()

    def left_own(g, k):
        def body(s):
            q = flip(s)
            left_z(g, k, q, mine(q)).wait_recv()
            left_x(g, k, q, mine(q)).start()
        loop(1, half, body)

    def left_other(g, k):
        loop(0, half, lambda s: left_x(g, k, s, theirs(s)).wait_recv())

    def pair_copy(i, k, q):
        return copy_t(sbuf.at[i, k, 0, q], precv.at[i, k, q], p_s.at[i, k, q], p_r.at[i, k, q], other)

    def pair_send(i, k):
        loop(0, half, lambda s: pair_copy(i, k, flip(half - 1 - s)).start())

    def s_copy(i, k, q, slot):
        return copy_t(sbuf.at[i, k, 1, q], srecv.at[i, k, slot], s_s.at[i, k, q], s_r.at[i, k, slot], mine(q))

    def join(i, k, s):
        q = flip(half - 1 - s)
        pair_copy(i, k, q).wait_recv()
        sbuf[i, k, 1, q] += precv[i, k, q]
        if s < half - 1:
            s_copy(i, k, q, z).start()

    def gq_copy(i, j, slot):
        return copy_t(grq.at[i, t, c], grq.at[i, slot, c], gq_s.at[i, j], gq_r.at[i, slot], j)

    def ga_copy(i, j, slot):
        return copy_c(grsum.at[i, c], grsum.at[i, slot], ga_s.at[i, j], ga_r.at[i, slot], j)

    def hq_copy(i, j, slot):
        return copy_c(glq.at[i, c, j], glq.at[i, slot, j], hq_s.at[i, j], hq_r.at[i, slot], j)

    def ht_copy(i, j, slot):
        return copy_t(glsum.at[i, t], glsum.at[i, slot], ht_s.at[i, j], ht_r.at[i, slot], j)

    def ha_copy(i, j, slot):
        return copy_c(glall.at[i, c], glall.at[i, slot], ha_s.at[i, j], ha_r.at[i, slot], j)

    def right_copy(j, slot):
        return copy_c(starts.at[:, pl.ds(lc, rc)], rg.at[0, slot], r_s.at[j], r_r.at[slot], j)

    def tc_copy(i, q):
        return copy_c(tsend.at[i, q], tcore.at[i, q], tc_s.at[i, q], tc_r.at[i, q], twin)

    def ty_copy(i, q, to, slot):
        return copy_c(tsum.at[i, y, q], tsum.at[i, slot, q], ty_s.at[i, q, to], ty_r.at[i, q, slot],
                      to * 2 + core)

    def rc_copy(i, q, who):
        at = q * 2 + who
        return copy_c(rg.at[i, q * 2 + core], rg.at[i, at], rc_s.at[i, q], rc_r.at[i, q], twin)

    def x_copy(j):
        at = pl.ds(pl.multiple_of(j * lc, lc), lc)
        return pltpu.make_async_copy(x_hbm.at[at], x.at[at], x_sem.at[j])

    barrier = pltpu.get_barrier_semaphore()
    loop(1, n, lambda s: pl.semaphore_signal(barrier, inc=1, device_id=(c, peer_t(s)), device_id_type=MESH))
    loop(1, m, lambda s: pl.semaphore_signal(barrier, inc=1, device_id=(peer_c(s), t), device_id_type=MESH))

    pl.semaphore_wait(barrier, n + m - 2)

    left_send(0, 0)
    loop(1, m, lambda s: right_copy(peer_c(s), c).start())
    for k in range(1, cut):
        left_send(0, k)
    loop(0, half, lambda s: x_copy(mine(s)).start())
    loop(0, half, lambda s: x_copy(theirs(s)).start())
    for k in range(cut):
        lg[0, k, t] = starts[:, k * lk:(k + 1) * lk]
    rg[0, c] = starts[:, lc:]

    rows = lax.broadcasted_iota(jnp.int32, (rank, rank), 0)
    cols = lax.broadcasted_iota(jnp.int32, (rank, rank), 1)
    ridge = jnp.where(rows == cols, RIDGE, 0.0).astype(jnp.float32)

    def when(cond, body):
        pl.when(cond)(body)

    def sent():
        loop(1, m, lambda s: right_copy(peer_c(s), c).wait_send())
        for i in range(ITERS):
            for k in range(cut):
                loop(0, half, lambda s: pair_copy(i, k, s).wait_send())
                loop(1, half, lambda s: s_copy(i, k, flip(s), z).wait_send())
            loop(1, n, lambda s: gq_copy(i, peer_t(s), t).wait_send())
            loop(1, m, lambda s: ga_copy(i, peer_c(s), c).wait_send())
            loop(1, m, lambda s: hq_copy(i, peer_c(s), c).wait_send())
            loop(1, n, lambda s: ht_copy(i, peer_t(s), t).wait_send())
            loop(1, m, lambda s: ha_copy(i, peer_c(s), c).wait_send())
            loop(0, ys, lambda q: tc_copy(i, q).wait_send())
            if i < ITERS - 1:
                for q in range(ys):
                    loop(1, ys, lambda s: ty_copy(i, q, peer_y(s), y).wait_send())
                loop(0, ys, lambda q: rc_copy(i + 1, q, core).wait_send())
        for g in range(ITERS + 1):
            for k in range(cut):
                loop(1, half, lambda s: left_z(g, k, flip(s), t).wait_send())
                loop(0, half, lambda s: left_x(g, k, s, t).wait_send())

    for i in range(ITERS):
        last = i == ITERS - 1

        def prepare(q, total):
            part = rg[i, q]
            both = stacked(part)
            high = both[:rank]
            low = both[rank:]
            at = pl.ds(pl.multiple_of(q * rc, rc), rc)
            rcat[:, at] = jnp.concatenate([high, high, low, low], axis=0).astype(jnp.bfloat16)
            rwide[at, :] = both.T.astype(jnp.bfloat16)
            term = outer_gram(part)
            return term if total is None else total + term

        total = None
        if i == 0:
            left_own(0, 0)
            loop(1, m, lambda s: right_copy(c, peer_c(s)).wait_recv())
            for q in range(m):
                total = prepare(q, total)
        else:
            for q in range(ys):
                total = prepare(q * 2 + core, total)
            for q in range(ys):
                rc_copy(i, q, 1 - core).wait_recv()
                total = prepare(q * 2 + 1 - core, total)
        grq[i, t] = packed(total).reshape(m, rank // 2 // m, 2 * rank)
        loop(1, n, lambda s: gq_copy(i, peer_t(s), t).start())

        def share():
            loop(1, n, lambda s: gq_copy(i, t, peer_t(s)).wait_recv())
            value = grq[i, 0, c]
            for q in range(1, n):
                value = value + grq[i, q, c]
            grsum[i, c] = value
            loop(1, m, lambda s: ga_copy(i, peer_c(s), c).start())

        def block_a(k, own):
            js = [q * 2 + side(own) for q in range(half)]
            ats = [pl.ds(pl.multiple_of(j * lc + k * lk, lk), lk) for j in js]
            twos = [stacked(lg[i, k, j]).T.astype(jnp.bfloat16) for j in js]
            lcat = jnp.concatenate(twos, axis=0)
            lcat = jnp.concatenate([lcat, lcat], axis=1)
            deep = half * lk
            sums = None
            for b in range(times // width):
                part = pl.ds(b * width, width)
                values = jnp.concatenate([x[at, part] for at in ats], axis=0)
                low_rank = dot(lcat, rcat[:, part])
                residue = values - low_rank
                kept = jnp.clip(residue, -LEVEL, LEVEL)
                if last:
                    outlier = residue - kept
                    for q, at in enumerate(ats):
                        x[at, part] = outlier[q * lk:(q + 1) * lk]
                high, low = split(low_rank + kept)
                clean[0, k, own, :, part] = high
                clean[1, k, own, :, part] = low
                term = dot(jnp.concatenate([high, low], axis=0), rwide[part, :])
                sums = term if sums is None else sums + term
            flat = (sums[:deep] + sums[deep:]).T
            flat = flat[:rank] + flat[rank:]
            for q in range(half):
                sbuf[i, k, own, q] = flat[:, q * lk:(q + 1) * lk]

        if i == 0:
            def step_a(s, carry):
                k, own = s // 2, 1 - s % 2
                when((own == 0) & (k < cut - 1), lambda: left_own(0, k + 1))
                when(own == 0, lambda: left_other(0, k))
                when(k == 0, lambda: loop(0, half, lambda q: x_copy(q * 2 + side(own)).wait()))
                block_a(k, own)
                when(own == 0, lambda: pair_send(0, k))
                when((own == 1) & (k == cut - 1), share)
                return carry
            lax.fori_loop(0, 2 * cut, step_a, 0)
            joins = [(k, s) for k in range(cut) for s in range(half)]
        else:
            early = half // 2

            def step_a(s, carry):
                k, own = s % cut, s // cut
                block_a(k, own)
                when(own == 0, lambda: pair_send(i, k))

                @pl.when((own == 1) & (k == 0))
                def _():
                    share()
                    for j in range(early):
                        join(i, 0, j)
                return carry
            lax.fori_loop(0, 2 * cut, step_a, 0)
            joins = [(k, s) for k in range(cut) for s in range(half) if (k, s) >= (0, early)]

        free = 0
        while free < len(joins) and joins[free][0] == 0 and i > 0:
            join(i, *joins[free])
            free += 1
        joins = joins[free:]
        loop(1, m, lambda s: ga_copy(i, c, peer_c(s)).wait_recv())
        gram = unpacked(grsum[i].reshape(rank // 2, 2 * rank)) + ridge
        per = max(4, rank // (len(joins) + 1) // 4 * 4)
        done = 0
        for k, s in joins:
            gram = pivots(gram, done, min(done + per, rank))
            done = min(done + per, rank)
            join(i, k, s)
        inv_r[...] = pivots(gram, done, rank)

        for k in range(cut):
            def add_s(s, value):
                q = flip(s)
                s_copy(i, k, z, q).wait_recv()
                return value + srecv[i, k, q]

            total = lax.fori_loop(1, half, add_s, sbuf[i, k, 1, z])
            piece = solved(inv_r[...], total)
            lg[i + 1, k, t] = piece
            left_send(i + 1, k)
            term = outer_gram(piece)
            gram = term if k == 0 else gram + term
            if last:
                lout[:, k * lk:(k + 1) * lk] = piece

        glq[i, c] = packed(gram).reshape(m, rank // 2 // m, 2 * rank)
        loop(1, m, lambda s: hq_copy(i, peer_c(s), c).start())
        acc[...] = jnp.zeros_like(acc)

        def share_chan():
            loop(1, m, lambda s: hq_copy(i, c, peer_c(s)).wait_recv())
            value = glq[i, 0, c]
            for q in range(1, m):
                value = value + glq[i, q, c]
            glsum[i, t] = value
            loop(1, n, lambda s: ht_copy(i, peer_t(s), t).start())

        def share_tm():
            loop(1, n, lambda s: ht_copy(i, t, peer_t(s)).wait_recv())
            value = glsum[i, 0]
            for q in range(1, n):
                value = value + glsum[i, q]
            glall[i, c] = value
            loop(1, m, lambda s: ha_copy(i, peer_c(s), c).start())

        def step_b(s, carry):
            k, own = s % cut, 1 - s // cut
            when(own == 1, lambda: left_own(i + 1, k))
            when(own == 0, lambda: left_other(i + 1, k))
            value = jnp.concatenate([lg[i + 1, k, q * 2 + side(own)] for q in range(half)], axis=1)
            both = stacked(value).astype(jnp.bfloat16)
            for b in range(times // width):
                part = pl.ds(b * width, width)
                acc[:, part] += dot(both, clean[0, k, own, :, part]) + dot(both, clean[1, k, own, :, part])
            when(s == 0, share_chan)
            when(s == cut, share_tm)
            return carry
        lax.fori_loop(0, 2 * cut, step_b, 0)

        def t_part(q, who):
            at = pl.ds(pl.multiple_of((q * 2 + who) * rc, rc), rc)
            return acc[:rank, at] + acc[rank:, at]

        def t_send(q):
            tsend[i, q] = t_part(q, 1 - core)
            tc_copy(i, q).start()

        def t_join(q):
            tsum[i, y, q] = t_part(q, core)
            tc_copy(i, q).wait_recv()
            tsum[i, y, q] += tcore[i, q]

        def over_y(s):
            q = peer_y(s)
            t_join(q)
            if last:
                when(s < ys, lambda: ty_copy(i, q, q, y).start())
            else:
                loop(1, ys, lambda v: ty_copy(i, q, peer_y(v), y).start())

        loop(1, ys + 1, lambda s: t_send(peer_y(s)))
        loop(1, ys + 1, over_y)

        loop(1, m, lambda s: ha_copy(i, c, peer_c(s)).wait_recv())
        inv_l = pivots(unpacked(glall[i].reshape(rank // 2, 2 * rank)) + ridge, 0, rank)

        def total_of(q):
            value = tsum[i, 0, q]
            for v in range(1, ys):
                value = value + tsum[i, v, q]
            return value

        if last:
            sent()
            loop(1, ys, lambda s: ty_copy(i, y, y, peer_y(s)).wait_recv())
            rout[...] = solved(inv_l, total_of(y))
        else:
            for q in range(ys):
                loop(1, ys, lambda s: ty_copy(i, q, y, peer_y(s)).wait_recv())
                rg[i + 1, q * 2 + core] = solved(inv_l, total_of(q))
                rc_copy(i + 1, q, core).start()

    loop(1, ys, lambda s: ty_copy(ITERS - 1, peer_y(s), peer_y(s), y).wait_send())


def store(parts, x, left, right, x_out, left_out, right_out, sem):
    rows = x.shape[0] // parts
    copies = [pltpu.make_async_copy(left, left_out, sem.at[parts]),
              pltpu.make_async_copy(right, right_out, sem.at[parts + 1])]
    for q in range(parts):
        at = pl.ds(q * rows, rows)
        copies.append(pltpu.make_async_copy(x.at[at], x_out.at[at], sem.at[q]))
    for copy in copies:
        copy.start()
    for copy in copies:
        copy.wait()


def shards(n, m, readings, channel_start, time_start):
    lc, rank = channel_start.shape
    rc = time_start.shape[0]
    rows, times = readings.shape
    cut = max(1, lc // LANES)
    lk, half, ys = lc // cut, n // 2, m // 2
    f32 = jnp.float32
    vmem = pl.BlockSpec(memory_space=pltpu.VMEM)
    hbm = pl.BlockSpec(memory_space=pltpu.HBM)
    dma = pltpu.SemaphoreType.DMA
    outliers, left, right = pl.pallas_call(
        functools.partial(kernel, n, m, cut, rc),
        out_shape=(jax.ShapeDtypeStruct((rows, times), f32),
                   jax.ShapeDtypeStruct((rank, lc), f32),
                   jax.ShapeDtypeStruct((rank, rc), f32)),
        in_specs=[hbm, vmem],
        out_specs=(vmem, vmem, vmem),
        scratch_shapes=[
            pltpu.VMEM((2, cut, 2, half * lk, times), jnp.bfloat16),
            pltpu.VMEM((ITERS + 1, cut, n, rank, lk), f32),
            pltpu.VMEM((ITERS, cut, 2, half, rank, lk), f32),
            pltpu.VMEM((ITERS, cut, half, rank, lk), f32),
            pltpu.VMEM((ITERS, cut, half, rank, lk), f32),
            pltpu.VMEM((ITERS, m, rank, rc), f32),
            pltpu.VMEM((ITERS, ys, rank, rc), f32),
            pltpu.VMEM((ITERS, ys, rank, rc), f32),
            pltpu.VMEM((ITERS, ys, ys, rank, rc), f32),
            pltpu.VMEM((ITERS, n, m, rank // 2 // m, 2 * rank), f32),
            pltpu.VMEM((ITERS, m, rank // 2 // m, 2 * rank), f32),
            pltpu.VMEM((ITERS, m, m, rank // 2 // m, 2 * rank), f32),
            pltpu.VMEM((ITERS, n, rank // 2 // m, 2 * rank), f32),
            pltpu.VMEM((ITERS, m, rank // 2 // m, 2 * rank), f32),
            pltpu.VMEM((4 * rank, times), jnp.bfloat16),
            pltpu.VMEM((times, 2 * rank), jnp.bfloat16),
            pltpu.VMEM((2 * rank, times), f32),
            pltpu.VMEM((rank, rank), f32),
            dma((ITERS + 1, cut, half)), dma((ITERS + 1, cut, half)), dma((ITERS + 1, cut, n)),
            dma((ITERS, cut, half)), dma((ITERS, cut, half)),
            dma((ITERS, cut, half)), dma((ITERS, cut, half)),
            dma((ITERS, n)), dma((ITERS, n)),
            dma((ITERS, m)), dma((ITERS, m)),
            dma((ITERS, m)), dma((ITERS, m)),
            dma((ITERS, n)), dma((ITERS, n)),
            dma((ITERS, m)), dma((ITERS, m)),
            dma((m,)), dma((m,)),
            dma((ITERS, ys)), dma((ITERS, ys)),
            dma((ITERS, ys, ys)), dma((ITERS, ys, ys)),
            dma((ITERS, ys)), dma((ITERS, ys)),
            dma((n,)),
        ],
        compiler_params=pltpu.CompilerParams(collective_id=0, has_side_effects=True,
                                             vmem_limit_bytes=42 * 1024 * 1024),
    )(readings, jnp.concatenate([channel_start.T, time_start.T], axis=1))
    parts = 8
    outliers, left, right = pl.pallas_call(
        functools.partial(store, parts),
        out_shape=(jax.ShapeDtypeStruct((rows, times), f32),
                   jax.ShapeDtypeStruct((rank, lc), f32),
                   jax.ShapeDtypeStruct((rank, rc), f32)),
        in_specs=[pl.BlockSpec(memory_space=pl.ANY)] * 3,
        out_specs=(hbm, hbm, hbm),
        scratch_shapes=[dma((parts + 2,))],
        compiler_params=pltpu.CompilerParams(vmem_limit_bytes=4 * 1024 * 1024),
    )(outliers, left, right)
    return outliers, left.T, right.T


def solution(mesh):
    n, m = mesh.shape["tm"], mesh.shape["chan"]
    specs = (P("chan", "tm"), P(("chan", "tm"), None), P(("tm", "chan"), None))
    return jax.shard_map(functools.partial(shards, n, m), mesh=mesh, in_specs=specs, out_specs=specs,
                         check_vma=False)
```
